32 devices in a mesh: blk: 16 (over z, y, x), rep: 2 (over core).
Axes of the slice: x: 2, y: 2, z: 4, core: 2. Of those that a mesh axis runs over, the one named last changes fastest.
Arguments:
- x_points: bfloat16 [16384, 512], P('blk'), may hold values from -8 to 8
- y_points: bfloat16 [16384, 512], P('blk'), may hold values from -8 to 8
- first_masses: float32 [16384], P('blk'), may hold values from 0.25 to 4
- second_masses: float32 [16384], P('blk'), may hold values from 0.25 to 4
- f_start: float32 [16384], P('blk'), may hold values from 0.55 to 20
- g_start: float32 [16384], P('blk'), may hold values from 0.55 to 20
- block_owner: int32 [32], replicated, may hold values from 0 to 31, as said below
- pair_list: int32 [128, 2], P(('blk', 'rep')), may hold values from -1 to 31, as said below
Outputs:
- f_final: float32 [16384], P('blk')
- g_final: float32 [16384], P('blk')
- mapped_x: bfloat16 [16384, 512], P('blk', 'rep')
- mapped_y: bfloat16 [16384, 512], P('blk', 'rep')
The draws below stay inside these ranges and needn't reach their ends.
Inputs may be any that keep to these rules, and one draw needn't show every extreme that they name: A permutation: block b of either cloud is stored at block position block_owner[b]. `pair_list`: the rows of one index i of blk (those of its devices along rep, in order) begin with 5 to 8 listed pairs and end with rows (-1, -1); some index holds the full 2 * 4 in every draw. A listed pair's first-cloud block has block_owner // 2 = i, its second-cloud block block_owner // 2 = i + d modulo the size of blk, with 1 <= |d| <= 2. No pair is listed twice.
All inputs are finite; a program needn't handle non-finite values.
Results may differ from the reference program's by a relative error of at most 0.0044.
Values may be sent and summed in bfloat16 or wider, within the bound.
No kernel may reach another device: no remote copies, remote signals or barrier semaphores. Data moves between devices by JAX's collectives and lax.ppermute only.
A program may use at most 128 MiB of HBM per device.

```python
import math
import jax
import jax.numpy as jnp
from jax import lax

D = 512
BLOCK_POINTS = 512
BLOCKS_PER_SHARD = 2
PAIR_DEV = 4
REACH = 2
BLOCK_TOTAL = 32
NPTS = 16384
PAIRS = 128
N_BLK = 16
N_REP = 2


def layout(key):
    folded = jax.random.fold_in(key, 7)
    key_owner, key_count, key_order, key_top = jax.random.split(folded, 4)
    owner_map = jax.random.permutation(key_owner, BLOCK_TOTAL).astype(jnp.int32)
    block_of = jnp.zeros((BLOCK_TOTAL,), jnp.int32).at[owner_map].set(jnp.arange(BLOCK_TOTAL, dtype=jnp.int32))
    capacity = PAIR_DEV * N_REP
    count_table = capacity - jnp.array([3, 2, 1, 0, 0], jnp.int32)
    counts = count_table[jax.random.randint(key_count, (N_BLK,), 0, 5)]
    busiest = jax.random.randint(key_top, (), 0, N_BLK)
    counts = counts.at[busiest].set(capacity)
    combos = BLOCKS_PER_SHARD * BLOCKS_PER_SHARD * 2 * REACH
    scores = jax.random.randint(key_order, (N_BLK, combos), 0, 1 << 16) * combos + jnp.arange(combos, dtype=jnp.int32)[None, :]
    ranking = jnp.argsort(scores, axis=1)[:, :capacity].astype(jnp.int32)
    x_pick = ranking % BLOCKS_PER_SHARD
    remainder = ranking // BLOCKS_PER_SHARD
    second = remainder % BLOCKS_PER_SHARD
    step_code = remainder // BLOCKS_PER_SHARD
    offset = jnp.where(step_code < REACH, step_code - REACH, step_code - REACH + 1)
    device = jnp.arange(N_BLK, dtype=jnp.int32)[:, None]
    x_slot = device * BLOCKS_PER_SHARD + x_pick
    y_slot = (device + offset) % N_BLK * BLOCKS_PER_SHARD + second
    is_live = jnp.arange(capacity, dtype=jnp.int32)[None, :] < counts[:, None]
    listed = jnp.stack([jnp.where(is_live, block_of[x_slot], -1), jnp.where(is_live, block_of[y_slot], -1)], axis=-1)
    return (owner_map, listed.reshape(N_BLK * capacity, 2).astype(jnp.int32))


def draw_block_owner(key, part):
    return layout(key)[0]


def draw_pair_list(key, part):
    return layout(key)[1]


def clouds(key):
    key_x, key_y = jax.random.split(jax.random.fold_in(key, 11), 2)
    x_cloud = jnp.clip(jax.random.normal(key_x, (NPTS, D), jnp.float32), -7.5, 7.5)
    y_cloud = jnp.clip(jax.random.normal(key_y, (NPTS, D), jnp.float32), -7.5, 7.5)
    return (x_cloud, y_cloud)


def draw_x_points(key, part):
    return clouds(key)[0].astype(jnp.bfloat16)


def draw_y_points(key, part):
    return clouds(key)[1].astype(jnp.bfloat16)


def potential(key, salt_value):
    values = jax.random.uniform(jax.random.fold_in(key, salt_value), (NPTS,), jnp.float32, 0.55, 0.9)
    return values


def draw_g_start(key, part):
    return potential(key, 17)


def draw_f_start(key, part):
    return potential(key, 19)


def steps_of(key, extent, shards, smallest, top_value):
    factor_of = 1.0
    for axis_at, blocks in shards:
        draws = jax.random.uniform(jax.random.fold_in(jax.random.fold_in(key, 6), axis_at), (blocks,), jnp.float32, smallest / len(shards), top_value / len(shards))
        factor_of = factor_of * jnp.repeat(jnp.exp(draws), extent[axis_at] // blocks).reshape((-1,) + (1,) * (len(extent) - 1 - axis_at))
    return factor_of


def setup_inputs(seed: int = 0) -> dict:
    keys = jax.random.split(jax.random.key(seed), 9)
    x_points = draw_x_points(jax.random.fold_in(keys[8], 71), 0)
    y_points = draw_y_points(jax.random.fold_in(keys[8], 71), 0)
    first_masses = jnp.clip(jnp.exp(math.log(4.0) - 2.7725887 * jax.random.uniform(keys[2], (NPTS,), jnp.float32) ** steps_of(keys[2], (NPTS,), ((0, 16),), -0.2, 0.2)), 0.25, 4.0)
    second_masses = jnp.clip(jnp.exp(math.log(4.0) - 2.7725887 * jax.random.uniform(keys[3], (NPTS,), jnp.float32) ** steps_of(keys[3], (NPTS,), ((0, 16),), -0.2, 0.2)), 0.25, 4.0)
    f_start = draw_f_start(jax.random.fold_in(keys[8], 71), 0)
    g_start = draw_g_start(jax.random.fold_in(keys[8], 71), 0)
    block_owner = draw_block_owner(jax.random.fold_in(keys[8], 71), 0)
    pair_list = draw_pair_list(jax.random.fold_in(keys[8], 71), 0)
    return dict(x_points=x_points, y_points=y_points, first_masses=first_masses, second_masses=second_masses, f_start=f_start, g_start=g_start, block_owner=block_owner, pair_list=pair_list)


entropic_epsilon = 0.05
floor_value = -1.0e30


def block_cost(x_block, y_block):
    x_wide = x_block.astype(jnp.float32)
    y_wide = y_block.astype(jnp.float32)
    x_square = jnp.sum(jnp.square(x_wide), axis=1)
    y_square = jnp.sum(jnp.square(y_wide), axis=1)
    inner_dot = jnp.dot(x_wide, y_wide.T)
    return (x_square[:, None] + y_square[None, :] - 2.0 * inner_dot) / D


def merge_rows(maxima, totals, slot_ids):
    highest = jnp.full((BLOCK_TOTAL, BLOCK_POINTS), floor_value, jnp.float32).at[slot_ids].max(maxima)
    scaled = totals * jnp.exp(maxima - highest[slot_ids])
    combined = jnp.zeros((BLOCK_TOTAL, BLOCK_POINTS), jnp.float32).at[slot_ids].add(scaled)
    return highest + jnp.log(combined)


def reference(x_points, y_points, first_masses, second_masses, f_start, g_start, block_owner, pair_list):
    is_live = pair_list[:, 0] >= 0
    first_id = jnp.where(is_live, pair_list[:, 0], 0).astype(jnp.int32)
    second_id = jnp.where(is_live, pair_list[:, 1], 0).astype(jnp.int32)
    home_slots = jnp.arange(BLOCK_TOTAL, dtype=jnp.int32)
    x_slot = jnp.concatenate([home_slots, block_owner[first_id]]).astype(jnp.int32)
    y_slot = jnp.concatenate([home_slots, block_owner[second_id]]).astype(jnp.int32)
    in_use = jnp.concatenate([jnp.ones((BLOCK_TOTAL,), jnp.bool_), is_live])
    x_blocks = x_points.reshape(BLOCK_TOTAL, BLOCK_POINTS, D)
    y_blocks = y_points.reshape(BLOCK_TOTAL, BLOCK_POINTS, D)
    entries = jnp.arange(BLOCK_TOTAL + PAIRS, dtype=jnp.int32)

    def make_cost(entry_index):
        return block_cost(x_blocks[x_slot[entry_index]], y_blocks[y_slot[entry_index]])

    cost_tiles = lax.map(make_cost, entries)
    first_log_mass = entropic_epsilon * jnp.log(first_masses.reshape(BLOCK_TOTAL, BLOCK_POINTS))
    second_log_mass = entropic_epsilon * jnp.log(second_masses.reshape(BLOCK_TOTAL, BLOCK_POINTS))

    def softmin_parts(first_block_start, second_block_start):
        def one_entry(packed):
            pair_cost_block, first_block_index, second_block_index, active = packed
            row_logits = (second_block_start[second_block_index][None, :] - pair_cost_block) / entropic_epsilon
            column_logits = (first_block_start[first_block_index][:, None] - pair_cost_block) / entropic_epsilon
            row_high = jnp.max(row_logits, axis=1)
            col_high = jnp.max(column_logits, axis=0)
            row_summed = jnp.sum(jnp.exp(row_logits - row_high[:, None]), axis=1)
            col_summed = jnp.sum(jnp.exp(column_logits - col_high[None, :]), axis=0)
            return (jnp.where(active, row_high, floor_value), jnp.where(active, row_summed, 0.0),
                    jnp.where(active, col_high, floor_value), jnp.where(active, col_summed, 0.0))

        row_high, row_summed, col_high, col_summed = lax.map(one_entry, (cost_tiles, x_slot, y_slot, in_use))
        return merge_rows(row_high, row_summed, x_slot), merge_rows(col_high, col_summed, y_slot)

    first_potential = f_start.reshape(BLOCK_TOTAL, BLOCK_POINTS)
    second_potential = g_start.reshape(BLOCK_TOTAL, BLOCK_POINTS)
    for sweep_count in range(2):
        row_logsumexp, column_logsumexp = softmin_parts(first_potential + first_log_mass, second_potential + second_log_mass)
        first_potential, second_potential = 0.5 * (first_potential - entropic_epsilon * row_logsumexp), 0.5 * (second_potential - entropic_epsilon * column_logsumexp)
    first_block_start = first_potential + first_log_mass
    second_block_start = second_potential + second_log_mass
    row_logsumexp, column_logsumexp = softmin_parts(first_block_start, second_block_start)

    def accumulate(carried, packed):
        x_sums, y_sums = carried
        pair_cost_block, first_block_index, second_block_index, active = packed
        row_factor = jnp.exp((second_block_start[second_block_index][None, :] - pair_cost_block) / entropic_epsilon - row_logsumexp[first_block_index][:, None])
        column_factor = jnp.exp((first_block_start[first_block_index][:, None] - pair_cost_block) / entropic_epsilon - column_logsumexp[second_block_index][None, :])
        row_factor = jnp.where(active, row_factor, 0.0).astype(jnp.bfloat16).astype(jnp.float32)
        column_factor = jnp.where(active, column_factor, 0.0).astype(jnp.bfloat16).astype(jnp.float32)
        add_x = jnp.dot(row_factor, y_blocks[second_block_index].astype(jnp.float32))
        add_y = jnp.dot(column_factor.T, x_blocks[first_block_index].astype(jnp.float32))
        return (x_sums.at[first_block_index].add(add_x), y_sums.at[second_block_index].add(add_y)), None

    zeros_sums = jnp.zeros((BLOCK_TOTAL, BLOCK_POINTS, D), jnp.float32)
    (x_sums, y_sums), unused = lax.scan(accumulate, (zeros_sums, zeros_sums), (cost_tiles, x_slot, y_slot, in_use))
    return (first_potential.reshape(NPTS), second_potential.reshape(NPTS),
            x_sums.reshape(NPTS, D).astype(jnp.bfloat16), y_sums.reshape(NPTS, D).astype(jnp.bfloat16))
```

```python
import functools
import math

import jax
import jax.numpy as jnp
from jax import lax
from jax.experimental import pallas as pl
from jax.experimental.pallas import tpu as pltpu
from jax.sharding import PartitionSpec as P


EPSILON = 0.05
LOG2E = math.log2(math.e)
SCALE = LOG2E / EPSILON
FLOOR = -1e30
LANES = 128
CHUNK = 64
F32 = jnp.float32
BF16 = jnp.bfloat16


def to_x(k):
    return k ^ 1


def to_y(k):
    return k ^ 2


def to_z(k):
    return k + 4 if k % 4 < 2 else k - 4


def to_z_back(k):
    return k - 4 if k % 4 < 2 else k + 4


def to_m(k):
    return k + 1 if k % 2 == 1 else k - 1


def to_z_direct(k):
    return k + 2 if k % 4 >= 2 else k - 2


def send(value, target):
    count = lax.axis_size("blk")
    return lax.ppermute(value, "blk", [(k, target(k) % count) for k in range(count)])


def send_each(value, target_first, target_second):
    count = lax.axis_size("blk")
    pairs = []
    for k in range(count):
        pairs.append((2 * k, 2 * (target_first(k) % count)))
        pairs.append((2 * k + 1, 2 * (target_second(k) % count) + 1))
    return lax.ppermute(value, ("blk", "rep"), pairs)


def swap(value):
    return lax.ppermute(value, "rep", [(0, 1), (1, 0)])


def exchange(packet):
    first = send_each(packet, to_x, to_y)
    second = send_each(packet, to_m, to_z_direct)
    mine = jnp.concatenate([first, second], 0)
    return mine, swap(mine)


def fold_tile(tile, offsets, high, summed, first_row, points):
    def step(c, _):
        rows = pl.ds(pl.multiple_of(c * CHUNK, CHUNK), CHUNK)
        held = pl.ds(pl.multiple_of(first_row + c * CHUNK, CHUNK), CHUNK)
        old = high[held, :]
        logits = [
            tile[rows, l * LANES : (l + 1) * LANES] + offsets[:, l * LANES : (l + 1) * LANES]
            for l in range(points // LANES)
        ]
        new = functools.reduce(jnp.maximum, logits, old)
        total = summed[held, :] * jnp.exp2(old - new)
        for z in logits:
            total = total + jnp.exp2(z - new)
        high[held, :] = new
        summed[held, :] = total
        return 0

    lax.fori_loop(0, points // CHUNK, step, 0)


def finish(high, summed, points, blocks):
    top = high[...]
    highest = jnp.max(top, axis=1, keepdims=True)
    total = jnp.sum(summed[...] * jnp.exp2(top - highest), axis=1, keepdims=True)
    column = highest + jnp.log2(total)
    wide = jnp.broadcast_to(column, top.shape)
    rows = [
        jnp.transpose(wide[b * points : (b + 1) * points, :])[0:1, :] for b in range(blocks)
    ]
    return column, jnp.concatenate(rows, 0)


def updated(logs, state):
    blocks = logs.shape[0]
    potential, norm, mass = (state[n * blocks : (n + 1) * blocks, :] for n in range(3))
    new = 0.5 * (potential - (logs - norm) * (1.0 / SCALE))
    return new, new * SCALE + mass - norm


def build_kernel(
    count, home, first, last, dim, points, blocks, flags, own, offsets, state, *rest
):
    rest = list(rest)
    carried = None if first else (rest.pop(0), rest.pop(0))
    sources = [rest.pop(0) for _ in range(count)]
    tiles_out = rest.pop(0)
    if last:
        packet_out = rest.pop(0)
    else:
        high_out, summed_out = rest.pop(0), rest.pop(0)
    other, tiles, high, summed, in_sem, out_sem = rest
    for n in range(count):
        pltpu.make_async_copy(sources[n], other.at[n], in_sem.at[n]).start()
    if first:
        high[...] = jnp.full_like(high, FLOOR)
        summed[...] = jnp.zeros_like(summed)
    else:
        high[...] = carried[0][...]
        summed[...] = carried[1][...]
    factor = 2.0 * SCALE / dim

    def block(n, _):
        pltpu.make_async_copy(sources[0], other.at[n], in_sem.at[n]).wait()

        def visit(p, _):
            t = n if home else n * blocks + p

            @pl.when(flags[n * blocks + p] > 0)
            def _():
                rows = pl.ds(pl.multiple_of(p * points, points), points)
                product = lax.dot_general(
                    own[rows, :], other[n], (((1,), (1,)), ((), ())), preferred_element_type=F32
                )
                tiles[t] = product * factor
                pltpu.make_async_copy(tiles.at[t], tiles_out.at[t], out_sem.at[t]).start()
                fold_tile(
                    tiles.at[t], offsets[pl.ds(n, 1), :], high, summed, p * points, points
                )

            return 0

        return lax.fori_loop(0, blocks, visit, 0)

    lax.fori_loop(0, count, block, 0)
    if last:
        _, logs = finish(high, summed, points, blocks)
        new, offset = updated(logs, state[...])
        packet_out[0:blocks, :] = new
        packet_out[blocks : 2 * blocks, :] = offset
    else:
        high_out[...] = high[...]
        summed_out[...] = summed[...]

    def drain(n, _):
        def one(p, _):
            t = n if home else n * blocks + p

            @pl.when(flags[n * blocks + p] > 0)
            def _():
                pltpu.make_async_copy(tiles.at[t], tiles_out.at[t], out_sem.at[t]).wait()

            return 0

        return lax.fori_loop(0, blocks, one, 0)

    lax.fori_loop(0, count, drain, 0)


def sweep_kernel(groups, apply, dim, points, blocks, flags, offsets, state, *rest):
    rest = list(rest)
    total_blocks = sum(count for count, _ in groups)
    kept = [rest.pop(0) for _ in groups]
    if apply:
        sources = [rest.pop(0) for _ in range(total_blocks)]
        keep_out, send_out = rest.pop(0), rest.pop(0)
        other, sums, tiles, high, summed, other_sem, sem = rest
    else:
        packet_out = rest.pop(0)
        tiles, high, summed, sem = rest
    base = 0
    for (count, home), source in zip(groups, kept):
        for n in range(count):
            for p in range(blocks):
                t = (base + n) * blocks + p

                @pl.when(flags[t] > 0)
                def _():
                    pltpu.make_async_copy(
                        source.at[n if home else n * blocks + p], tiles.at[t], sem.at[t]
                    ).start()

        base += count
    if apply:
        for n in range(total_blocks):
            pltpu.make_async_copy(sources[n], other.at[n], other_sem.at[n]).start()
    high[...] = jnp.full_like(high, FLOOR)
    summed[...] = jnp.zeros_like(summed)

    def fold(t, _):
        n, p = t // blocks, t % blocks

        @pl.when(flags[t] > 0)
        def _():
            pltpu.make_async_copy(kept[0].at[0], tiles.at[t], sem.at[t]).wait()
            fold_tile(tiles.at[t], offsets[pl.ds(n, 1), :], high, summed, p * points, points)

        return 0

    lax.fori_loop(0, total_blocks * blocks, fold, 0)
    column, logs = finish(high, summed, points, blocks)
    if not apply:
        new, offset = updated(logs, state[...])
        packet_out[0:blocks, :] = new
        packet_out[blocks : 2 * blocks, :] = offset
        return
    high[...] = jnp.broadcast_to(column, high.shape)
    sums[...] = jnp.zeros_like(sums)

    def weigh(t, _):
        n, p = t // blocks, t % blocks

        @pl.when(t % blocks == 0)
        def _():
            pltpu.make_async_copy(sources[0], other.at[n], other_sem.at[n]).wait()

        @pl.when(flags[t] > 0)
        def _():
            rows = pl.ds(pl.multiple_of(p * points, points), points)
            logits = tiles[t] + offsets[pl.ds(n, 1), :]
            weights = jnp.exp2(logits - high[rows, 0:1]).astype(BF16)
            sums[rows, :] += jnp.dot(weights, other[n], preferred_element_type=F32)

        return 0

    lax.fori_loop(0, total_blocks * blocks, weigh, 0)
    half = sums.shape[1] // 2
    role = flags[total_blocks * blocks]
    low, up = sums[:, :half].astype(BF16), sums[:, half:].astype(BF16)

    @pl.when(role == 0)
    def _():
        keep_out[...] = low
        send_out[...] = up

    @pl.when(role != 0)
    def _():
        keep_out[...] = up
        send_out[...] = low


VMEM_SPEC = pl.BlockSpec(memory_space=pltpu.VMEM)
ANY_SPEC = pl.BlockSpec(memory_space=pl.ANY)
SMEM_SPEC = pl.BlockSpec(memory_space=pltpu.SMEM)


def cost(tiles, points, dim, products):
    area = points * points
    return pl.CostEstimate(
        flops=tiles * area * (2 * dim * products + 8),
        transcendentals=tiles * area,
        bytes_accessed=tiles * area * 4,
    )


def build(flags, own, offsets, state, sources, carried, home, last):
    count = len(sources)
    points, dim = sources[0].shape
    rows = own.shape[0]
    blocks = rows // points
    tile_count = count if home else count * blocks
    lanes = jax.ShapeDtypeStruct((rows, LANES), F32)
    outs = [jax.ShapeDtypeStruct((tile_count, points, points), F32)]
    if last:
        outs.append(jax.ShapeDtypeStruct((2 * blocks, points), F32))
    else:
        outs += [lanes, lanes]
    carried = list(carried or ())
    return pl.pallas_call(
        functools.partial(
            build_kernel, count, home, not carried, last, dim, points, blocks
        ),
        out_shape=outs,
        in_specs=[SMEM_SPEC] + [VMEM_SPEC] * (3 + len(carried)) + [ANY_SPEC] * count,
        out_specs=[ANY_SPEC] + [VMEM_SPEC] * (len(outs) - 1),
        scratch_shapes=[
            pltpu.VMEM((count, points, dim), BF16),
            pltpu.VMEM((tile_count, points, points), F32),
            pltpu.VMEM((rows, LANES), F32),
            pltpu.VMEM((rows, LANES), F32),
            pltpu.SemaphoreType.DMA((count,)),
            pltpu.SemaphoreType.DMA((tile_count,)),
        ],
        cost_estimate=cost(tile_count, points, dim, 1),
    )(flags, own, offsets, state, *carried, *sources)


def sweep(flags, offsets, state, kept, groups, sources, rows, dim):
    points = kept[0].shape[1]
    blocks = rows // points
    total_blocks = sum(count for count, _ in groups)
    slots = total_blocks * blocks
    apply = sources is not None
    scratch = [
        pltpu.VMEM((slots, points, points), F32),
        pltpu.VMEM((rows, LANES), F32),
        pltpu.VMEM((rows, LANES), F32),
    ]
    if apply:
        outs = [jax.ShapeDtypeStruct((rows, dim // 2), BF16)] * 2
        scratch = (
            [pltpu.VMEM((total_blocks, points, dim), BF16), pltpu.VMEM((rows, dim), F32)]
            + scratch
            + [pltpu.SemaphoreType.DMA((total_blocks,))]
        )
    else:
        outs = [jax.ShapeDtypeStruct((2 * blocks, points), F32)]
    return pl.pallas_call(
        functools.partial(sweep_kernel, groups, apply, dim, points, blocks),
        out_shape=outs,
        in_specs=[SMEM_SPEC, VMEM_SPEC, VMEM_SPEC]
        + [ANY_SPEC] * (len(kept) + (total_blocks if apply else 0)),
        out_specs=[VMEM_SPEC] * len(outs),
        scratch_shapes=scratch + [pltpu.SemaphoreType.DMA((slots,))],
        cost_estimate=cost(slots, points, dim, 1 if apply else 0),
    )(flags, offsets, state, *kept, *(sources or ()))


ORDER = ("H0", "H1", "Y0", "X1", "X0", "Y1", "Z0", "Z1", "M0", "M1")
GROUPS = ((2, True), (2, False), (3, False), (3, False))


def per_device(
    x_points, y_points, first_masses, second_masses, f_start, g_start, block_owner, pair_list
):
    index = lax.axis_index("blk")
    count = lax.axis_size("blk")
    role = lax.axis_index("rep")
    row_role = role == 0
    rows, dim = x_points.shape
    total = block_owner.shape[0]
    blocks = total // count
    points = rows // blocks
    place = index % 4

    own = jnp.where(row_role, x_points, y_points)
    home = [
        jnp.where(
            row_role,
            y_points[b * points : (b + 1) * points],
            x_points[b * points : (b + 1) * points],
        )
        for b in range(blocks)
    ]

    x1 = send(home[1], to_x)
    y0 = send(home[0], to_y)
    x0 = send(home[0], to_x)
    y1 = send(home[1], to_y)
    outer = (place == 0) | (place == 3)
    z0 = send(y0, to_z)
    w1 = send(x1, to_z_back)
    m0 = send(jnp.where(outer, y0, z0), to_x)
    m1 = send(jnp.where(outer, x1, w1), to_y)
    z1 = send(y1, to_z)
    arrived = dict(
        H0=home[0], H1=home[1], X0=x0, X1=x1, Y0=y0, Y1=y1, Z0=z0, Z1=z1, M0=m0, M1=m1
    )

    pairs = lax.all_gather(pair_list, "rep", tiled=True)
    ids = jnp.arange(total, dtype=jnp.int32)
    slots = jnp.sum(
        jnp.where(pairs[:, :, None] == ids[None, None, :], block_owner[None, None, :], 0), axis=2
    )
    ahead = (slots[:, 1] // blocks - index + 2) % count
    code = (ahead * blocks + slots[:, 0] % blocks) * blocks + slots[:, 1] % blocks
    code = jnp.where(pairs[:, 0] >= 0, code, -1)
    listed = jnp.any(
        code[:, None] == jnp.arange(points, dtype=jnp.int32)[None, :], axis=0
    ).astype(F32)

    def norm_of(a):
        return (jnp.sum(jnp.square(a.astype(F32)), axis=1) * (SCALE / dim)).reshape(blocks, points)

    shape = (blocks, points)
    x_norm, y_norm = norm_of(x_points), norm_of(y_points)
    x_mass, y_mass = (jnp.log2(a.reshape(shape)) for a in (first_masses, second_masses))
    f, g = f_start.reshape(shape), g_start.reshape(shape)
    state_f = jnp.concatenate([f, x_norm, x_mass], 0)
    state_g = jnp.concatenate([g, y_norm, y_mass], 0)
    state = jnp.where(row_role, state_f, state_g)

    def packed(f_offset, g_offset, extra):
        return jnp.concatenate([f_offset, g_offset, extra], 0)

    f_offset, g_offset = f * SCALE + x_mass - x_norm, g * SCALE + y_mass - y_norm
    extra = jnp.broadcast_to(listed[None, :], (8 - 2 * blocks, points))
    packet = packed(f_offset, g_offset, extra)
    mine, theirs = exchange(packet)

    def by_source(packet, mine, theirs):
        low, up = jnp.where(row_role, mine, theirs), jnp.where(row_role, theirs, mine)
        return dict(H=packet, X=low[:8], M=low[8:], Y=up[:8], Z=up[8:])

    def other_offsets(sources):
        picked = []
        for name in ORDER:
            a = sources[name[0]]
            b = int(name[1])
            picked.append(jnp.where(row_role, a[blocks + b], a[b]))
        picked += [picked[0]] * (16 - len(picked))
        return jnp.stack(picked, 0)

    def offsets_of(offsets, start, size):
        padded = offsets[start : start + size]
        return jnp.concatenate([padded, jnp.zeros((8 - size, points), F32)], 0)

    sources = by_source(packet, mine, theirs)
    offsets = other_offsets(sources)

    even = place % 2 == 0
    lower = place < 2
    distance = dict(
        X=jnp.where(even, 1, -1),
        M=jnp.where(even, -1, 1),
        Y=jnp.where(lower, 2, -2),
        Z=jnp.where(lower, -2, 2),
    )
    wide = 32
    spots, tables = [], []
    for name in ORDER:
        d = distance.get(name[0], 0)
        b = int(name[1])
        table = sources[name[0]][2 * blocks, :wide]
        table = jnp.where(row_role, packet[2 * blocks, :wide], table)
        for p in range(blocks):
            tables.append(table)
            as_row = ((d + 2) * blocks + p) * blocks + b
            as_col = ((2 - d) * blocks + b) * blocks + p
            spots.append(jnp.where(row_role, as_row, as_col))
    found = jnp.where(
        jnp.stack(spots)[:, None] == jnp.arange(wide, dtype=jnp.int32)[None, :],
        jnp.stack(tables),
        0.0,
    )
    flags = jnp.sum(found, axis=1).astype(jnp.int32)
    at_home = [1 if n == p else 0 for n in range(blocks) for p in range(blocks)]
    flags = jnp.concatenate(
        [jnp.array(at_home, jnp.int32), flags[len(at_home) :], role.astype(jnp.int32)[None]]
    )

    kept = []
    carried = None
    start = 0
    for n, (size, is_home) in enumerate(GROUPS):
        last = n == len(GROUPS) - 1
        if is_home:
            group_flags = jnp.array(
                [1 if p == b else 0 for b in range(blocks) for p in range(blocks)], jnp.int32
            )
            group_offsets = jnp.where(row_role, g_offset, f_offset)
            group_offsets = jnp.concatenate(
                [group_offsets, jnp.zeros((8 - blocks, points), F32)], 0
            )
        else:
            group_flags = flags[start * blocks : (start + size) * blocks]
            group_offsets = offsets_of(offsets, start, size)
        out = build(
            group_flags,
            own,
            group_offsets,
            state,
            [arrived[name] for name in ORDER[start : start + size]],
            carried,
            is_home,
            last,
        )
        kept.append(out[0])
        if last:
            result = out[1]
        else:
            carried = (out[1], out[2])
        start += size

    def next_packet(result):
        back = swap(result)
        f_part, g_part = jnp.where(row_role, result, back), jnp.where(row_role, back, result)
        packet = packed(
            f_part[blocks:], g_part[blocks:], jnp.concatenate([f_part[:blocks], g_part[:blocks]], 0)
        )
        return packet

    def next_state(result):
        return jnp.concatenate([result[:blocks], state[blocks:]], 0)

    packet = next_packet(result)
    offsets = other_offsets(by_source(packet, *exchange(packet)))
    (result,) = sweep(flags, offsets, next_state(result), kept, GROUPS, None, rows, dim)
    packet = next_packet(result)
    offsets = other_offsets(by_source(packet, *exchange(packet)))
    stay, leave = sweep(
        flags,
        offsets,
        next_state(result),
        kept,
        GROUPS,
        [arrived[name] for name in ORDER],
        rows,
        dim,
    )
    came = swap(leave)
    return (
        packet[2 * blocks : 3 * blocks].reshape(rows),
        packet[3 * blocks : 4 * blocks].reshape(rows),
        jnp.where(row_role, stay, came),
        jnp.where(row_role, came, stay),
    )


def solution(mesh):
    placed = (
        P("blk", None),
        P("blk", None),
        P("blk"),
        P("blk"),
        P("blk"),
        P("blk"),
        P(),
        P(("blk", "rep"), None),
    )
    return jax.shard_map(
        per_device,
        mesh=mesh,
        in_specs=placed,
        out_specs=(P("blk"), P("blk"), P("blk", "rep"), P("blk", "rep")),
        check_vma=False,
    )
```

```python
import functools
import math

import jax
import jax.numpy as jnp
from jax import lax
from jax.experimental import pallas as pl
from jax.experimental.pallas import tpu as pltpu
from jax.sharding import PartitionSpec as P


EPSILON = 0.05
LOG2E = math.log2(math.e)
SCALE = LOG2E / EPSILON
FLOOR = -1e30
LANES = 128
CHUNK = 64
F32 = jnp.float32
BF16 = jnp.bfloat16


def to_x(k):
    return k ^ 1


def to_y(k):
    return k ^ 2


def to_z(k):
    return k + 4 if k % 4 < 2 else k - 4


def to_z_back(k):
    return k - 4 if k % 4 < 2 else k + 4


def to_m(k):
    return k + 1 if k % 2 == 1 else k - 1


def to_z_direct(k):
    return k + 2 if k % 4 >= 2 else k - 2


def send(value, target):
    count = lax.axis_size("blk")
    return lax.ppermute(value, "blk", [(k, target(k) % count) for k in range(count)])


def send_across(value, target):
    count = lax.axis_size("blk")
    pairs = []
    for k in range(count):
        pairs.append((2 * k, 2 * (target(k) % count) + 1))
        pairs.append((2 * k + 1, 2 * (target(k) % count)))
    return lax.ppermute(value, ("blk", "rep"), pairs)


def swap(value):
    return lax.ppermute(value, "rep", [(0, 1), (1, 0)])


def exchange(packet):
    came = {}
    for source, target in (("M", to_m), ("Z", to_z_direct), ("X", to_x), ("Y", to_y)):
        came[source] = send_across(packet, target)
    came["H"] = swap(packet)
    return came


def fold_tile(tile, offsets, high, summed, first_row, points):
    def step(c, _):
        rows = pl.ds(pl.multiple_of(c * CHUNK, CHUNK), CHUNK)
        held = pl.ds(pl.multiple_of(first_row + c * CHUNK, CHUNK), CHUNK)
        old = high[held, :]
        logits = [
            tile[rows, l * LANES : (l + 1) * LANES] + offsets[:, l * LANES : (l + 1) * LANES]
            for l in range(points // LANES)
        ]
        new = functools.reduce(jnp.maximum, logits, old)
        total = summed[held, :] * jnp.exp2(old - new)
        for z in logits:
            total = total + jnp.exp2(z - new)
        high[held, :] = new
        summed[held, :] = total
        return 0

    lax.fori_loop(0, points // CHUNK, step, 0)


def finish(high, summed, points, blocks):
    top = high[...]
    highest = jnp.max(top, axis=1, keepdims=True)
    total = jnp.sum(summed[...] * jnp.exp2(top - highest), axis=1, keepdims=True)
    column = highest + jnp.log2(total)
    wide = jnp.broadcast_to(column, top.shape)
    rows = [
        jnp.transpose(wide[b * points : (b + 1) * points, :])[0:1, :] for b in range(blocks)
    ]
    return column, jnp.concatenate(rows, 0)


def updated(logs, state):
    blocks = logs.shape[0]
    potential, norm, mass = (state[n * blocks : (n + 1) * blocks, :] for n in range(3))
    new = 0.5 * (potential - (logs - norm) * (1.0 / SCALE))
    return new, new * SCALE + mass - norm


def gather_offsets(names, packets, offsets):
    for n, name in enumerate(names):
        b = int(name[1])
        offsets[n : n + 1, :] = packets[name[0]][b : b + 1, :]


def build_kernel(
    names, packet_names, first, last, dim, points, blocks, flags, x_ref, y_ref, state, *rest
):
    rest = list(rest)
    count, home = len(names), names[0][0] == "H"
    packets = {name: rest.pop(0) for name in packet_names}
    carried = None if first else (rest.pop(0), rest.pop(0))
    sources = [rest.pop(0) for _ in range(count)]
    tiles_out = rest.pop(0)
    if last:
        packet_out = rest.pop(0)
    else:
        high_out, summed_out = rest.pop(0), rest.pop(0)
    own, other, tiles, high, summed, offsets, own_sem, in_sem, out_sem = rest
    role = flags[count * blocks]

    @pl.when(role == 0)
    def _():
        pltpu.make_async_copy(x_ref, own, own_sem).start()

    @pl.when(role != 0)
    def _():
        pltpu.make_async_copy(y_ref, own, own_sem).start()

    for n in range(count):
        pltpu.make_async_copy(sources[n], other.at[n], in_sem.at[n]).start()
    if first:
        high[...] = jnp.full_like(high, FLOOR)
        summed[...] = jnp.zeros_like(summed)
    else:
        high[...] = carried[0][...]
        summed[...] = carried[1][...]
    factor = 2.0 * SCALE / dim
    gather_offsets(names, packets, offsets)
    pltpu.make_async_copy(x_ref, own, own_sem).wait()

    def block(n, _):
        pltpu.make_async_copy(sources[0], other.at[n], in_sem.at[n]).wait()

        def visit(p, _):
            t = n if home else n * blocks + p

            @pl.when(flags[n * blocks + p] > 0)
            def _():
                rows = pl.ds(pl.multiple_of(p * points, points), points)
                product = lax.dot_general(
                    own[rows, :], other[n], (((1,), (1,)), ((), ())), preferred_element_type=F32
                )
                tiles[t] = product * factor
                pltpu.make_async_copy(tiles.at[t], tiles_out.at[t], out_sem.at[t]).start()
                fold_tile(
                    tiles.at[t], offsets[pl.ds(n, 1), :], high, summed, p * points, points
                )

            return 0

        return lax.fori_loop(0, blocks, visit, 0)

    lax.fori_loop(0, count, block, 0)
    if last:
        _, logs = finish(high, summed, points, blocks)
        new, offset = updated(logs, state[...])
        packet_out[0:blocks, :] = offset
        packet_out[blocks : 2 * blocks, :] = new
    else:
        high_out[...] = high[...]
        summed_out[...] = summed[...]

    def drain(n, _):
        def one(p, _):
            t = n if home else n * blocks + p

            @pl.when(flags[n * blocks + p] > 0)
            def _():
                pltpu.make_async_copy(tiles.at[t], tiles_out.at[t], out_sem.at[t]).wait()

            return 0

        return lax.fori_loop(0, blocks, one, 0)

    lax.fori_loop(0, count, drain, 0)


def sweep_kernel(names, groups, packet_names, apply, points, blocks, flags, state, *rest):
    rest = list(rest)
    total_blocks = len(names)
    packets = {name: rest.pop(0) for name in packet_names}
    kept = [rest.pop(0) for _ in groups]
    if apply:
        sources = [rest.pop(0) for _ in range(total_blocks)]
        keep_out, send_out = rest.pop(0), rest.pop(0)
        other, sums, tiles, high, summed, offsets, other_sem, sem = rest
    else:
        packet_out = rest.pop(0)
        tiles, high, summed, offsets, sem = rest
    base = 0
    for group, source in zip(groups, kept):
        count, home = len(group), group[0][0] == "H"
        for n in range(count):
            for p in range(blocks):
                t = (base + n) * blocks + p

                @pl.when(flags[t] > 0)
                def _():
                    pltpu.make_async_copy(
                        source.at[n if home else n * blocks + p], tiles.at[t], sem.at[t]
                    ).start()

        base += count
    if apply:
        for n in range(total_blocks):
            pltpu.make_async_copy(sources[n], other.at[n], other_sem.at[n]).start()
    high[...] = jnp.full_like(high, FLOOR)
    summed[...] = jnp.zeros_like(summed)
    gather_offsets(names, packets, offsets)

    def fold(t, _):
        n, p = t // blocks, t % blocks

        @pl.when(flags[t] > 0)
        def _():
            pltpu.make_async_copy(kept[0].at[0], tiles.at[t], sem.at[t]).wait()
            fold_tile(tiles.at[t], offsets[pl.ds(n, 1), :], high, summed, p * points, points)

        return 0

    lax.fori_loop(0, total_blocks * blocks, fold, 0)
    column, logs = finish(high, summed, points, blocks)
    if not apply:
        new, offset = updated(logs, state[...])
        packet_out[0:blocks, :] = offset
        packet_out[blocks : 2 * blocks, :] = new
        return
    high[...] = jnp.broadcast_to(column, high.shape)
    sums[...] = jnp.zeros_like(sums)

    def weigh(t, _):
        n, p = t // blocks, t % blocks

        @pl.when(t % blocks == 0)
        def _():
            pltpu.make_async_copy(sources[0], other.at[n], other_sem.at[n]).wait()

        @pl.when(flags[t] > 0)
        def _():
            rows = pl.ds(pl.multiple_of(p * points, points), points)
            logits = tiles[t] + offsets[pl.ds(n, 1), :]
            weights = jnp.exp2(logits - high[rows, 0:1]).astype(BF16)
            sums[rows, :] += jnp.dot(weights, other[n], preferred_element_type=F32)

        return 0

    lax.fori_loop(0, total_blocks * blocks, weigh, 0)
    half = sums.shape[1] // 2
    role = flags[total_blocks * blocks]
    low, up = sums[:, :half].astype(BF16), sums[:, half:].astype(BF16)

    @pl.when(role == 0)
    def _():
        keep_out[...] = low
        send_out[...] = up

    @pl.when(role != 0)
    def _():
        keep_out[...] = up
        send_out[...] = low


VMEM_SPEC = pl.BlockSpec(memory_space=pltpu.VMEM)
ANY_SPEC = pl.BlockSpec(memory_space=pl.ANY)
SMEM_SPEC = pl.BlockSpec(memory_space=pltpu.SMEM)


def cost(tiles, points, dim, products):
    area = points * points
    return pl.CostEstimate(
        flops=tiles * area * (2 * dim * products + 8),
        transcendentals=tiles * area,
        bytes_accessed=tiles * area * 4,
    )


def build(names, flags, x_points, y_points, state, packets, sources, carried, last):
    count, home = len(names), names[0][0] == "H"
    points, dim = sources[0].shape
    rows = x_points.shape[0]
    blocks = rows // points
    tile_count = count if home else count * blocks
    lanes = jax.ShapeDtypeStruct((rows, LANES), F32)
    outs = [jax.ShapeDtypeStruct((tile_count, points, points), F32)]
    if last:
        outs.append(jax.ShapeDtypeStruct((2 * blocks, points), F32))
    else:
        outs += [lanes, lanes]
    carried = list(carried or ())
    packet_names = sorted({name[0] for name in names})
    return pl.pallas_call(
        functools.partial(
            build_kernel, names, packet_names, not carried, last, dim, points, blocks
        ),
        out_shape=outs,
        in_specs=[SMEM_SPEC, ANY_SPEC, ANY_SPEC]
        + [VMEM_SPEC] * (1 + len(packet_names) + len(carried))
        + [ANY_SPEC] * count,
        out_specs=[ANY_SPEC] + [VMEM_SPEC] * (len(outs) - 1),
        scratch_shapes=[
            pltpu.VMEM((rows, dim), BF16),
            pltpu.VMEM((count, points, dim), BF16),
            pltpu.VMEM((tile_count, points, points), F32),
            pltpu.VMEM((rows, LANES), F32),
            pltpu.VMEM((rows, LANES), F32),
            pltpu.VMEM((16, points), F32),
            pltpu.SemaphoreType.DMA,
            pltpu.SemaphoreType.DMA((count,)),
            pltpu.SemaphoreType.DMA((tile_count,)),
        ],
        cost_estimate=cost(tile_count, points, dim, 1),
    )(flags, x_points, y_points, state, *[packets[n] for n in packet_names], *carried, *sources)


def sweep(names, groups, flags, state, packets, kept, sources, rows, dim):
    points = kept[0].shape[1]
    blocks = rows // points
    total_blocks = len(names)
    slots = total_blocks * blocks
    apply = sources is not None
    scratch = [
        pltpu.VMEM((slots, points, points), F32),
        pltpu.VMEM((rows, LANES), F32),
        pltpu.VMEM((rows, LANES), F32),
        pltpu.VMEM((16, points), F32),
    ]
    if apply:
        outs = [jax.ShapeDtypeStruct((rows, dim // 2), BF16)] * 2
        scratch = (
            [pltpu.VMEM((total_blocks, points, dim), BF16), pltpu.VMEM((rows, dim), F32)]
            + scratch
            + [pltpu.SemaphoreType.DMA((total_blocks,))]
        )
    else:
        outs = [jax.ShapeDtypeStruct((2 * blocks, points), F32)]
    packet_names = sorted(packets)
    return pl.pallas_call(
        functools.partial(sweep_kernel, names, groups, packet_names, apply, points, blocks),
        out_shape=outs,
        in_specs=[SMEM_SPEC] + [VMEM_SPEC] * (1 + len(packet_names))
        + [ANY_SPEC] * (len(kept) + (total_blocks if apply else 0)),
        out_specs=[VMEM_SPEC] * len(outs),
        scratch_shapes=scratch + [pltpu.SemaphoreType.DMA((slots,))],
        cost_estimate=cost(slots, points, dim, 1 if apply else 0),
    )(flags, state, *[packets[n] for n in packet_names], *kept, *(sources or ()))


GROUPS = (("H0", "H1"), ("Y0", "X1"), ("X0", "Y1", "Z0"), ("Z1", "M0", "M1"))
ORDER = sum(GROUPS, ())


def per_device(
    x_points, y_points, first_masses, second_masses, f_start, g_start, block_owner, pair_list
):
    index = lax.axis_index("blk")
    count = lax.axis_size("blk")
    role = lax.axis_index("rep")
    row_role = role == 0
    rows, dim = x_points.shape
    total = block_owner.shape[0]
    blocks = total // count
    points = rows // blocks
    place = index % 4

    home = [
        jnp.where(
            row_role,
            y_points[b * points : (b + 1) * points],
            x_points[b * points : (b + 1) * points],
        )
        for b in range(blocks)
    ]

    y0 = send(home[0], to_y)
    x1 = send(home[1], to_x)
    x0 = send(home[0], to_x)
    y1 = send(home[1], to_y)
    outer = (place == 0) | (place == 3)
    z0 = send(y0, to_z)
    w1 = send(x1, to_z_back)
    m0 = send(jnp.where(outer, y0, z0), to_x)
    m1 = send(jnp.where(outer, x1, w1), to_y)
    z1 = send(y1, to_z)
    arrived = dict(
        H0=home[0], H1=home[1], X0=x0, X1=x1, Y0=y0, Y1=y1, Z0=z0, Z1=z1, M0=m0, M1=m1
    )

    wide = 32
    pair_rest = swap(pair_list)
    pairs = jnp.concatenate([pair_list, pair_rest], 0)
    ids = jnp.arange(total, dtype=jnp.int32)
    slots = jnp.sum(
        jnp.where(pairs[:, :, None] == ids[None, None, :], block_owner[None, None, :], 0), axis=2
    )
    ahead = (slots[:, 1] // blocks - index + 2) % count
    code = (ahead * blocks + slots[:, 0] % blocks) * blocks + slots[:, 1] % blocks
    code = jnp.where(pairs[:, 0] >= 0, code, -1)
    listed = jnp.any(
        code[:, None] == jnp.arange(points, dtype=jnp.int32)[None, :], axis=0
    ).astype(F32)

    shape = (blocks, points)
    own = jnp.where(row_role, x_points, y_points)
    norm = (jnp.sum(jnp.square(own.astype(F32)), axis=1) * (SCALE / dim)).reshape(shape)
    potential = jnp.where(row_role, f_start, g_start).reshape(shape)
    mass = jnp.log2(jnp.where(row_role, first_masses, second_masses)).reshape(shape)
    state = jnp.concatenate([potential, norm, mass], 0)

    packet = jnp.concatenate(
        [potential * SCALE + mass - norm, jnp.broadcast_to(listed[None, :], shape)], 0
    )
    packets = exchange(packet)

    even = place % 2 == 0
    lower = place < 2
    distance = dict(
        X=jnp.where(even, 1, -1),
        M=jnp.where(even, -1, 1),
        Y=jnp.where(lower, 2, -2),
        Z=jnp.where(lower, -2, 2),
    )
    spots, tables = [], []
    for name in ORDER:
        d = distance.get(name[0], 0)
        b = int(name[1])
        table = jnp.where(
            row_role, packet[blocks, :wide], packets[name[0]][blocks, :wide]
        )
        for p in range(blocks):
            tables.append(table)
            as_row = ((d + 2) * blocks + p) * blocks + b
            as_col = ((2 - d) * blocks + b) * blocks + p
            spots.append(jnp.where(row_role, as_row, as_col))
    found = jnp.where(
        jnp.stack(spots)[:, None] == jnp.arange(wide, dtype=jnp.int32)[None, :],
        jnp.stack(tables),
        0.0,
    )
    flags = jnp.sum(found, axis=1).astype(jnp.int32)
    role_flag = role.astype(jnp.int32)[None]
    at_home = jnp.array([n == p for n in range(blocks) for p in range(blocks)], jnp.int32)
    flags = jnp.concatenate([at_home, flags[blocks * blocks :], role_flag])

    kept = []
    carried = None
    start = 0
    for n, names in enumerate(GROUPS):
        last = n == len(GROUPS) - 1
        if n == 0:
            some = at_home
        else:
            some = flags[start * blocks : (start + len(names)) * blocks]
        out = build(
            names,
            jnp.concatenate([some, role_flag]),
            x_points,
            y_points,
            state,
            packets,
            [arrived[name] for name in names],
            carried,
            last,
        )
        kept.append(out[0])
        if last:
            packet = out[1]
        else:
            carried = (out[1], out[2])
        start += len(names)

    def now(packet):
        return jnp.concatenate([packet[blocks:], state[blocks:]], 0)

    packets = exchange(packet)
    (packet,) = sweep(ORDER, GROUPS, flags, now(packet), packets, kept, None, rows, dim)
    packets = exchange(packet)
    stay, leave = sweep(
        ORDER,
        GROUPS,
        flags,
        now(packet),
        packets,
        kept,
        [arrived[name] for name in ORDER],
        rows,
        dim,
    )
    came = swap(leave)
    mine, theirs = packet[blocks:], packets["H"][blocks:]
    return (
        jnp.where(row_role, mine, theirs).reshape(rows),
        jnp.where(row_role, theirs, mine).reshape(rows),
        jnp.where(row_role, stay, came),
        jnp.where(row_role, came, stay),
    )


def solution(mesh):
    placed = (
        P("blk", None),
        P("blk", None),
        P("blk"),
        P("blk"),
        P("blk"),
        P("blk"),
        P(),
        P(("blk", "rep"), None),
    )
    return jax.shard_map(
        per_device,
        mesh=mesh,
        in_specs=placed,
        out_specs=(P("blk"), P("blk"), P("blk", "rep"), P("blk", "rep")),
        check_vma=False,
    )
```

```python
import functools
import math

import jax
import jax.numpy as jnp
from jax import lax
from jax.experimental import pallas as pl
from jax.experimental.pallas import tpu as pltpu
from jax.sharding import PartitionSpec as P


EPSILON = 0.05
LOG2E = math.log2(math.e)
SCALE = LOG2E / EPSILON
FLOOR = -1e30
LANES = 128
CHUNK = 64
UNROLL = 8
EXTRA = 16
F32 = jnp.float32
BF16 = jnp.bfloat16


def to_x(k):
    return k ^ 1


def to_y(k):
    return k ^ 2


def to_z(k):
    return k + 4 if k % 4 < 2 else k - 4


def to_z_back(k):
    return k - 4 if k % 4 < 2 else k + 4


def to_m(k):
    return k + 1 if k % 2 == 1 else k - 1


def to_z_direct(k):
    return k + 2 if k % 4 >= 2 else k - 2


def send(value, target, places=range(4)):
    count = lax.axis_size("blk")
    pairs = [(k, target(k) % count) for k in range(count) if k % 4 in places]
    return lax.ppermute(value, "blk", pairs)


def send_across(value, target):
    count = lax.axis_size("blk")
    pairs = []
    for k in range(count):
        pairs.append((2 * k, 2 * (target(k) % count) + 1))
        pairs.append((2 * k + 1, 2 * (target(k) % count)))
    return lax.ppermute(value, ("blk", "rep"), pairs)


def swap(value):
    return lax.ppermute(value, "rep", [(0, 1), (1, 0)])


def exchange(packet):
    came = {}
    for source, target in (("M", to_m), ("Z", to_z_direct), ("X", to_x), ("Y", to_y)):
        came[source] = send_across(packet, target)
    came["H"] = swap(packet)
    return came


def fold_tile(tile, offsets, high, summed, first_row, points):
    def step(c, _):
        rows = pl.ds(pl.multiple_of(c * CHUNK, CHUNK), CHUNK)
        held = pl.ds(pl.multiple_of(first_row + c * CHUNK, CHUNK), CHUNK)
        old = high[held, :]
        logits = [
            tile[rows, l * LANES : (l + 1) * LANES] + offsets[:, l * LANES : (l + 1) * LANES]
            for l in range(points // LANES)
        ]
        new = functools.reduce(jnp.maximum, logits, old)
        total = summed[held, :] * jnp.exp2(old - new)
        for z in logits:
            total = total + jnp.exp2(z - new)
        high[held, :] = new
        summed[held, :] = total
        return 0

    lax.fori_loop(0, points // CHUNK, step, 0, unroll=UNROLL)


def finish(high, summed, points, blocks):
    top = high[...]
    highest = jnp.max(top, axis=1, keepdims=True)
    total = jnp.sum(summed[...] * jnp.exp2(top - highest), axis=1, keepdims=True)
    column = highest + jnp.log2(total)
    wide = jnp.broadcast_to(column, top.shape)
    rows = [
        jnp.transpose(wide[b * points : (b + 1) * points, :])[0:1, :] for b in range(blocks)
    ]
    return column, jnp.concatenate(rows, 0)


def updated(logs, state):
    blocks = logs.shape[0]
    potential, norm, mass = (state[n * blocks : (n + 1) * blocks, :] for n in range(3))
    new = 0.5 * (potential - (logs - norm) * (1.0 / SCALE))
    return new, new * SCALE + mass - norm


def each_role(first, second):
    role = lax.axis_index("rep")
    pl.when(role == 0)(first)
    pl.when(role != 0)(second)


def row_norm(block, factor):
    wide = block.astype(F32)
    square = wide * wide
    part = functools.reduce(
        jnp.add, [square[:, l : l + LANES] for l in range(0, square.shape[1], LANES)]
    )
    return jnp.sum(jnp.transpose(part), axis=0, keepdims=True) * factor


def in_three(value):
    first = value.astype(BF16)
    rest = value - first.astype(F32)
    second = rest.astype(BF16)
    return first, second, (rest - second.astype(F32)).astype(BF16)


def one_row(line, b, points):
    per = points // LANES
    return jnp.concatenate([line[b * per + l : b * per + l + 1, :] for l in range(per)], 1)


def prepare_kernel(
    dim, points, blocks, count, owner, pairs, pair_rest, f, g, first, second, x_ref, y_ref, *rest
):
    outs, held, in_sem, out_sem = rest[:blocks], *rest[blocks:]

    def fetch(source):
        for b in range(blocks):
            pltpu.make_async_copy(
                source.at[pl.ds(b * points, points), :],
                held.at[b, pl.ds(0, points), :],
                in_sem.at[b],
            ).start()

    each_role(lambda: fetch(y_ref), lambda: fetch(x_ref))
    role = lax.axis_index("rep")
    index = lax.axis_index("blk")
    lane = lax.broadcasted_iota(jnp.int32, (1, points), 1)
    listed = jnp.zeros((1, points), jnp.bool_)
    for ref in (pairs, pair_rest):
        for row in range(ref.shape[0]):
            live = ref[row, 0] >= 0
            own = owner[jnp.maximum(ref[row, 0], 0)]
            other = owner[jnp.maximum(ref[row, 1], 0)]
            ahead = lax.rem(other // blocks - index + 2 + count, count)
            code = (ahead * blocks + lax.rem(own, blocks)) * blocks + lax.rem(other, blocks)
            listed = jnp.logical_or(listed, lane == jnp.where(live, code, -1))
    listed = jnp.where(listed, 1.0, 0.0).astype(F32)
    zeros = jnp.zeros((EXTRA - 4, points), F32)
    for b in range(blocks):
        pltpu.make_async_copy(
            x_ref.at[pl.ds(0, points), :], held.at[b, pl.ds(0, points), :], in_sem.at[b]
        ).wait()
        norm = row_norm(held[b, 0:points, :], SCALE / dim)
        potential = jnp.where(role == 0, one_row(g, b, points), one_row(f, b, points))
        mass = jnp.where(role == 0, one_row(second, b, points), one_row(first, b, points))
        terms = in_three(potential * SCALE + jnp.log2(mass) - norm)
        extra = jnp.concatenate([term.astype(F32) for term in terms] + [listed, zeros], 0)
        held[b, points : points + EXTRA, :] = extra.astype(BF16)
        pltpu.make_async_copy(held.at[b], outs[b], out_sem.at[b]).start()
    for b in range(blocks):
        pltpu.make_async_copy(held.at[b], outs[b], out_sem.at[b]).wait()


def spot_of(name, p, blocks):
    place = lax.rem(lax.axis_index("blk"), 4)
    even = lax.rem(place, 2) == 0
    lower = place < 2
    d = {
        "X": jnp.where(even, 1, -1),
        "M": jnp.where(even, -1, 1),
        "Y": jnp.where(lower, 2, -2),
        "Z": jnp.where(lower, -2, 2),
    }[name[0]]
    b = int(name[1])
    return ((d + 2) * blocks + p) * blocks + b, ((2 - d) * blocks + b) * blocks + p


def build_kernel(names, first, last, dim, points, blocks, listing, x_ref, y_ref, *rest):
    rest = list(rest)
    count, home = len(names), names[0][0] == "H"
    state = [rest.pop(0) for _ in range(4)] if first else rest.pop(0)
    carried = None if first else (rest.pop(0), rest.pop(0))
    sources = [rest.pop(0) for _ in range(count)]
    flags, tiles_out = rest.pop(0), rest.pop(0)
    if first:
        state_out = rest.pop(0)
    if last:
        packet_out = rest.pop(0)
    else:
        high_out, summed_out = rest.pop(0), rest.pop(0)
    own, other, tiles, high, summed, offsets, own_sem, lane_sem, in_sem, out_sem = rest

    def fetch(source):
        pltpu.make_async_copy(source, own, own_sem).start()

    each_role(lambda: fetch(x_ref), lambda: fetch(y_ref))
    for n in range(count):
        pltpu.make_async_copy(sources[n], other.at[n], in_sem.at[n]).start()
    if first:
        high[...] = jnp.full_like(high, FLOOR)
        summed[...] = jnp.zeros_like(summed)
    else:
        pltpu.make_async_copy(carried[0], high, lane_sem.at[0]).start()
        pltpu.make_async_copy(carried[1], summed, lane_sem.at[1]).start()
    factor = 2.0 * SCALE / dim
    role = lax.axis_index("rep")
    lane = lax.broadcasted_iota(jnp.int32, (1, LANES), 1)
    for n, name in enumerate(names):
        pltpu.make_async_copy(sources[n], other.at[n], in_sem.at[n]).wait()
        extra = other[n, points : points + EXTRA, :].astype(F32)
        offsets[n : n + 1, :] = extra[0:1, :] + extra[1:2, :] + extra[2:3, :]
        for p in range(blocks):
            if home:
                flags[n * blocks + p] = jnp.int32(p == int(name[1]))
                continue
            as_row, as_col = spot_of(name, p, blocks)
            row = jnp.where(role == 0, listing[0:1, :], extra[3:4, 0:LANES])
            spot = jnp.where(role == 0, as_row, as_col)
            found = jnp.max(jnp.where(lane == spot, row, 0.0))
            flags[n * blocks + p] = found.astype(jnp.int32)
    pltpu.make_async_copy(x_ref, own, own_sem).wait()
    if not first:
        pltpu.make_async_copy(carried[0], high, lane_sem.at[0]).wait()
        pltpu.make_async_copy(carried[1], summed, lane_sem.at[1]).wait()

    def slot(t):
        return t // blocks if home else t

    def visit(t, _):
        n, p = t // blocks, lax.rem(t, blocks)

        @pl.when(flags[t] > 0)
        def _():
            rows = pl.ds(pl.multiple_of(p * points, points), points)
            tile = tiles.at[slot(t)]
            product = lax.dot_general(
                own[rows, :],
                other[n, 0:points, :],
                (((1,), (1,)), ((), ())),
                preferred_element_type=F32,
            )
            tile[...] = product * factor
            pltpu.make_async_copy(tile, tiles_out.at[slot(t)], out_sem.at[slot(t)]).start()
            fold_tile(tile, offsets[pl.ds(n, 1), :], high, summed, p * points, points)

        return 0

    lax.fori_loop(0, count * blocks, visit, 0)
    if first:
        norms = [
            row_norm(own[b * points : (b + 1) * points, :], SCALE / dim) for b in range(blocks)
        ]
        for b in range(blocks):
            potential = jnp.where(
                role == 0, one_row(state[0], b, points), one_row(state[1], b, points)
            )
            mass = jnp.where(
                role == 0, one_row(state[2], b, points), one_row(state[3], b, points)
            )
            state_out[b : b + 1, :] = potential
            state_out[2 * blocks + b : 2 * blocks + b + 1, :] = jnp.log2(mass)
            state_out[blocks + b : blocks + b + 1, :] = norms[b]
    if last:
        _, logs = finish(high, summed, points, blocks)
        new, offset = updated(logs, state[...])
        packet_out[0:blocks, :] = offset
        packet_out[blocks : 2 * blocks, :] = new
    else:
        pltpu.make_async_copy(high, high_out, lane_sem.at[0]).start()
        pltpu.make_async_copy(summed, summed_out, lane_sem.at[1]).start()

    def drain(t, _):
        @pl.when(flags[t] > 0)
        def _():
            pltpu.make_async_copy(
                tiles.at[slot(t)], tiles_out.at[slot(t)], out_sem.at[slot(t)]
            ).wait()

        return 0

    lax.fori_loop(0, count * blocks, drain, 0)
    if not last:
        pltpu.make_async_copy(high, high_out, lane_sem.at[0]).wait()
        pltpu.make_async_copy(summed, summed_out, lane_sem.at[1]).wait()


def sweep_kernel(names, groups, packet_names, apply, points, blocks, state, before, *rest):
    rest = list(rest)
    total_blocks = len(names)
    some_flags = [rest.pop(0) for _ in groups]
    packets = {name: rest.pop(0) for name in packet_names}
    kept = [rest.pop(0) for _ in groups]
    if apply:
        sources = [rest.pop(0) for _ in range(total_blocks)]
        potential_outs = (rest.pop(0), rest.pop(0))
        mapped_outs = (rest.pop(0), rest.pop(0))
        send_out = rest.pop(0)
        other, sums, halves, other_sem, half_sem = (rest.pop(0) for _ in range(5))
    else:
        packet_out = rest.pop(0)
    tiles, high, summed, offsets, flags, sem = rest
    base = 0
    for group, group_flags, source in zip(groups, some_flags, kept):
        count, home = len(group), group[0][0] == "H"
        for n in range(count):
            for p in range(blocks):
                t = (base + n) * blocks + p
                flags[t] = group_flags[n * blocks + p]

                @pl.when(flags[t] > 0)
                def _():
                    pltpu.make_async_copy(
                        source.at[n if home else n * blocks + p], tiles.at[t], sem.at[t]
                    ).start()

        base += count
    if apply:
        for n in range(total_blocks):
            pltpu.make_async_copy(
                sources[n].at[pl.ds(0, points), :], other.at[n], other_sem.at[n]
            ).start()
    high[...] = jnp.full_like(high, FLOOR)
    summed[...] = jnp.zeros_like(summed)
    for n, name in enumerate(names):
        b = int(name[1])
        offsets[n : n + 1, :] = packets[name[0]][b : b + 1, :]

    def fold(t, _):
        n, p = t // blocks, lax.rem(t, blocks)

        @pl.when(flags[t] > 0)
        def _():
            pltpu.make_async_copy(kept[0].at[0], tiles.at[t], sem.at[t]).wait()
            fold_tile(tiles.at[t], offsets[pl.ds(n, 1), :], high, summed, p * points, points)

        return 0

    lax.fori_loop(0, total_blocks * blocks, fold, 0)
    column, logs = finish(high, summed, points, blocks)
    if not apply:
        now = jnp.concatenate([before[blocks : 2 * blocks, :], state[blocks:, :]], 0)
        new, offset = updated(logs, now)
        packet_out[0:blocks, :] = offset
        packet_out[blocks : 2 * blocks, :] = new
        return
    high[...] = jnp.broadcast_to(column, high.shape)
    sums[...] = jnp.zeros_like(sums)
    role = lax.axis_index("rep")
    mine, theirs = before[blocks : 2 * blocks, :], packets["H"][blocks : 2 * blocks, :]
    for out, value in zip(
        potential_outs,
        (jnp.where(role == 0, mine, theirs), jnp.where(role == 0, theirs, mine)),
    ):
        per = points // LANES
        for row in range(out.shape[0]):
            b, l = row // per, row % per
            out[row : row + 1, :] = value[b : b + 1, l * LANES : (l + 1) * LANES]

    def weigh(t, _):
        n, p = t // blocks, lax.rem(t, blocks)

        @pl.when(p == 0)
        def _():
            pltpu.make_async_copy(
                sources[0].at[pl.ds(0, points), :], other.at[n], other_sem.at[n]
            ).wait()

        @pl.when(flags[t] > 0)
        def _():
            rows = pl.ds(pl.multiple_of(p * points, points), points)
            logits = tiles[t] + offsets[pl.ds(n, 1), :]
            weights = jnp.exp2(logits - high[rows, 0:1]).astype(BF16)
            sums[rows, :] += jnp.dot(weights, other[n], preferred_element_type=F32)

        return 0

    lax.fori_loop(0, total_blocks * blocks, weigh, 0)
    half = sums.shape[1] // 2
    for part in range(2):
        halves[part] = sums[:, part * half : (part + 1) * half].astype(BF16)

    def put(stay, out, leave):
        copies = (
            pltpu.make_async_copy(halves.at[stay], out, half_sem.at[0]),
            pltpu.make_async_copy(halves.at[leave], send_out, half_sem.at[1]),
        )
        for copy in copies:
            copy.start()
        for copy in copies:
            copy.wait()

    each_role(lambda: put(0, mapped_outs[0], 1), lambda: put(1, mapped_outs[1], 0))


def place_kernel(came, x_in, y_in, x_out, y_out, sem):
    def put(out):
        copy = pltpu.make_async_copy(came, out, sem)
        copy.start()
        copy.wait()

    each_role(lambda: put(y_out), lambda: put(x_out))


VMEM_SPEC = pl.BlockSpec(memory_space=pltpu.VMEM)
ANY_SPEC = pl.BlockSpec(memory_space=pl.ANY)
SMEM_SPEC = pl.BlockSpec(memory_space=pltpu.SMEM)


def cost(tiles, points, dim, products):
    area = points * points
    return pl.CostEstimate(
        flops=tiles * area * (2 * dim * products + 8),
        transcendentals=tiles * area,
        bytes_accessed=tiles * area * 4,
    )


def prepare(owner, pairs, pair_rest, vectors, x_points, y_points, points, count):
    rows, dim = x_points.shape
    blocks = rows // points
    payload = (points + EXTRA, dim)
    return pl.pallas_call(
        functools.partial(prepare_kernel, dim, points, blocks, count),
        out_shape=[jax.ShapeDtypeStruct(payload, BF16)] * blocks,
        in_specs=[SMEM_SPEC] * 3 + [VMEM_SPEC] * 4 + [ANY_SPEC] * 2,
        out_specs=[ANY_SPEC] * blocks,
        scratch_shapes=[
            pltpu.VMEM((blocks,) + payload, BF16),
            pltpu.SemaphoreType.DMA((blocks,)),
            pltpu.SemaphoreType.DMA((blocks,)),
        ],
    )(owner, pairs, pair_rest, *vectors, x_points, y_points)


def build(names, listing, x_points, y_points, state, sources, carried, last, points):
    count, home = len(names), names[0][0] == "H"
    rows, dim = x_points.shape
    blocks = rows // points
    tile_count = count if home else count * blocks
    lanes = jax.ShapeDtypeStruct((rows, LANES), F32)
    outs = [
        jax.ShapeDtypeStruct((count * blocks,), jnp.int32),
        jax.ShapeDtypeStruct((tile_count, points, points), F32),
    ]
    out_specs = [SMEM_SPEC, ANY_SPEC]
    if home:
        outs.append(jax.ShapeDtypeStruct((3 * blocks, points), F32))
        out_specs.append(VMEM_SPEC)
    if last:
        outs.append(jax.ShapeDtypeStruct((2 * blocks, points), F32))
        out_specs.append(VMEM_SPEC)
    else:
        outs += [lanes, lanes]
        out_specs += [ANY_SPEC] * 2
    carried = list(carried or ())
    return pl.pallas_call(
        functools.partial(build_kernel, names, home, last, dim, points, blocks),
        out_shape=outs,
        in_specs=[VMEM_SPEC, ANY_SPEC, ANY_SPEC]
        + [VMEM_SPEC] * len(state)
        + [ANY_SPEC] * (len(carried) + count),
        out_specs=out_specs,
        scratch_shapes=[
            pltpu.VMEM((rows, dim), BF16),
            pltpu.VMEM((count, points + EXTRA, dim), BF16),
            pltpu.VMEM((tile_count, points, points), F32),
            pltpu.VMEM((rows, LANES), F32),
            pltpu.VMEM((rows, LANES), F32),
            pltpu.VMEM((16, points), F32),
            pltpu.SemaphoreType.DMA,
            pltpu.SemaphoreType.DMA((2,)),
            pltpu.SemaphoreType.DMA((count,)),
            pltpu.SemaphoreType.DMA((tile_count,)),
        ],
        cost_estimate=cost(tile_count, points, dim, 1),
    )(listing, x_points, y_points, *state, *carried, *sources)


def sweep(names, groups, state, before, flags, packets, kept, sources, rows, dim):
    points = kept[0].shape[1]
    blocks = rows // points
    total_blocks = len(names)
    slots = total_blocks * blocks
    apply = sources is not None
    scratch = []
    if apply:
        half = jax.ShapeDtypeStruct((rows, dim // 2), BF16)
        line = jax.ShapeDtypeStruct((rows // LANES, LANES), F32)
        outs = [line, line, half, half, half]
        out_specs = [VMEM_SPEC] * 2 + [ANY_SPEC] * 3
        scratch = [
            pltpu.VMEM((total_blocks, points, dim), BF16),
            pltpu.VMEM((rows, dim), F32),
            pltpu.VMEM((2, rows, dim // 2), BF16),
            pltpu.SemaphoreType.DMA((total_blocks,)),
            pltpu.SemaphoreType.DMA((2,)),
        ]
    else:
        outs = [jax.ShapeDtypeStruct((2 * blocks, points), F32)]
        out_specs = [VMEM_SPEC]
    scratch += [
        pltpu.VMEM((slots, points, points), F32),
        pltpu.VMEM((rows, LANES), F32),
        pltpu.VMEM((rows, LANES), F32),
        pltpu.VMEM((16, points), F32),
        pltpu.SMEM((slots,), jnp.int32),
        pltpu.SemaphoreType.DMA((slots,)),
    ]
    packet_names = sorted(packets)
    return pl.pallas_call(
        functools.partial(sweep_kernel, names, groups, packet_names, apply, points, blocks),
        out_shape=outs,
        in_specs=[VMEM_SPEC] * 2
        + [SMEM_SPEC] * len(flags)
        + [VMEM_SPEC] * len(packet_names)
        + [ANY_SPEC] * (len(kept) + (total_blocks if apply else 0)),
        out_specs=out_specs,
        scratch_shapes=scratch,
        cost_estimate=cost(slots, points, dim, 1 if apply else 0),
    )(state, before, *flags, *[packets[n] for n in packet_names], *kept, *(sources or ()))


def placed_beside(came, x_part, y_part):
    shape = jax.ShapeDtypeStruct(came.shape, came.dtype)
    return pl.pallas_call(
        place_kernel,
        out_shape=[shape, shape],
        in_specs=[VMEM_SPEC] + [ANY_SPEC] * 2,
        out_specs=[ANY_SPEC] * 2,
        scratch_shapes=[pltpu.SemaphoreType.DMA],
        input_output_aliases={1: 0, 2: 1},
    )(came, x_part, y_part)


GROUPS = (("H0", "H1"), ("Y0", "X1"), ("X0", "Y1", "Z0"), ("Z1", "M0", "M1"))
ORDER = sum(GROUPS, ())


def per_device(
    x_points, y_points, first_masses, second_masses, f_start, g_start, block_owner, pair_list
):
    count = lax.axis_size("blk")
    rows, dim = x_points.shape
    blocks = block_owner.shape[0] // count
    points = rows // blocks
    place = lax.axis_index("blk") % 4
    vectors = [
        a.reshape(rows // LANES, LANES) for a in (f_start, g_start, first_masses, second_masses)
    ]
    pair_rest = swap(pair_list)
    home = prepare(block_owner, pair_list, pair_rest, vectors, x_points, y_points, points, count)

    y0 = send(home[0], to_y)
    x1 = send(home[1], to_x)
    x0 = send(home[0], to_x)
    y1 = send(home[1], to_y)
    outer = (place == 0) | (place == 3)
    z0 = send(y0, to_z)
    w1 = send(x1, to_z_back, (1, 2))
    m0 = send(jnp.where(outer, y0, z0), to_x)
    m1 = send(jnp.where(outer, x1, w1), to_y)
    z1 = send(y1, to_z)
    arrived = dict(
        H0=home[0], H1=home[1], X0=x0, X1=x1, Y0=y0, Y1=y1, Z0=z0, Z1=z1, M0=m0, M1=m1
    )
    listing = home[0][points + 3 : points + 4, :LANES].astype(F32)

    kept, flags = [], []
    carried, state = None, vectors
    for n, names in enumerate(GROUPS):
        last = n == len(GROUPS) - 1
        out = build(
            names,
            listing,
            x_points,
            y_points,
            state,
            [arrived[name] for name in names],
            carried,
            last,
            points,
        )
        flags.append(out[0])
        kept.append(out[1])
        if n == 0:
            state = [out[2]]
        if last:
            packet = out[-1]
        else:
            carried = out[-2:]

    (state,) = state
    packets = exchange(packet)
    (packet,) = sweep(ORDER, GROUPS, state, packet, flags, packets, kept, None, rows, dim)
    packets = exchange(packet)
    f, g, x_part, y_part, leave = sweep(
        ORDER,
        GROUPS,
        state,
        packet,
        flags,
        packets,
        kept,
        [arrived[name] for name in ORDER],
        rows,
        dim,
    )
    mapped_x, mapped_y = placed_beside(swap(leave), x_part, y_part)
    return f.reshape(rows), g.reshape(rows), mapped_x, mapped_y


def solution(mesh):
    placed = (
        P("blk", None),
        P("blk", None),
        P("blk"),
        P("blk"),
        P("blk"),
        P("blk"),
        P(),
        P(("blk", "rep"), None),
    )
    return jax.shard_map(
        per_device,
        mesh=mesh,
        in_specs=placed,
        out_specs=(P("blk"), P("blk"), P("blk", "rep"), P("blk", "rep")),
        check_vma=False,
    )
```

```python
import functools
import math

import jax
import jax.numpy as jnp
from jax import lax
from jax.experimental import pallas as pl
from jax.experimental.pallas import tpu as pltpu
from jax.sharding import PartitionSpec as P


EPSILON = 0.05
LOG2E = math.log2(math.e)
SCALE = LOG2E / EPSILON
FLOOR = -1e30
LANES = 128
CHUNK = 64
EXTRA = 16
BUILD_LIMIT = 12 << 20
SWEEP_LIMIT = 8 << 20
APPLY_LIMIT = 18 << 20
F32 = jnp.float32
BF16 = jnp.bfloat16


def to_x(k):
    return k ^ 1


def to_y(k):
    return k ^ 2


def to_z(k):
    return k + 4 if k % 4 < 2 else k - 4


def to_z_back(k):
    return k - 4 if k % 4 < 2 else k + 4


def to_m(k):
    return k + 1 if k % 2 == 1 else k - 1


def to_z_direct(k):
    return k + 2 if k % 4 >= 2 else k - 2


def send(value, target, places=range(4)):
    count = lax.axis_size("blk")
    pairs = [(k, target(k) % count) for k in range(count) if k % 4 in places]
    return lax.ppermute(value, "blk", pairs)


def send_across(value, target):
    count = lax.axis_size("blk")
    pairs = []
    for k in range(count):
        pairs.append((2 * k, 2 * (target(k) % count) + 1))
        pairs.append((2 * k + 1, 2 * (target(k) % count)))
    return lax.ppermute(value, ("blk", "rep"), pairs)


def swap(value):
    return lax.ppermute(value, "rep", [(0, 1), (1, 0)])


def in_vmem(value):
    return pltpu.with_memory_space_constraint(value, pltpu.VMEM)


def exchange(packet):
    came = {}
    for source, target in (("M", to_m), ("Z", to_z_direct), ("X", to_x), ("Y", to_y)):
        came[source] = send_across(packet, target)
    came["H"] = swap(packet)
    return came


def fold_tile(tile, offsets, high, summed, first_row, peaks=None, powers=None):
    lanes = [slice(l, l + LANES) for l in range(0, tile.shape[1], LANES)]
    for c in range(0, tile.shape[0], CHUNK):
        rows = slice(c, c + CHUNK)
        held = pl.ds(pl.multiple_of(first_row + c, CHUNK), CHUNK)
        old = high[held, :]
        logits = [tile[rows, l] + offsets[:, l] for l in lanes]
        new = functools.reduce(jnp.maximum, logits, old)
        total = summed[held, :] * jnp.exp2(old - new)
        for l, z in zip(lanes, logits):
            e = jnp.exp2(z - new)
            total = total + e
            if peaks is not None:
                powers[rows, l] = e
        high[held, :] = new
        summed[held, :] = total
        if peaks is not None:
            peaks[rows, :] = new


def finish(high, summed, points, blocks):
    top = high[...]
    highest = jnp.max(top, axis=1, keepdims=True)
    total = jnp.sum(summed[...] * jnp.exp2(top - highest), axis=1, keepdims=True)
    column = highest + jnp.log2(total)
    wide = jnp.broadcast_to(column, top.shape)
    rows = [
        jnp.transpose(wide[b * points : (b + 1) * points, :])[0:1, :] for b in range(blocks)
    ]
    return column, jnp.concatenate(rows, 0)


def updated(logs, state):
    blocks = logs.shape[0]
    potential, norm, mass = (state[n * blocks : (n + 1) * blocks, :] for n in range(3))
    new = 0.5 * (potential - (logs - norm) * (1.0 / SCALE))
    return new, new * SCALE + mass - norm


def each_role(first, second):
    role = lax.axis_index("rep")
    pl.when(role == 0)(first)
    pl.when(role != 0)(second)


def row_norm(block, factor):
    wide = block.astype(F32)
    square = wide * wide
    part = functools.reduce(
        jnp.add, [square[:, l : l + LANES] for l in range(0, square.shape[1], LANES)]
    )
    return jnp.sum(jnp.transpose(part), axis=0, keepdims=True) * factor


def in_three(value):
    first = value.astype(BF16)
    rest = value - first.astype(F32)
    second = rest.astype(BF16)
    return first, second, (rest - second.astype(F32)).astype(BF16)


def one_row(line, b, points):
    per = points // LANES
    return jnp.concatenate([line[b * per + l : b * per + l + 1, :] for l in range(per)], 1)


def prepare_kernel(
    dim, points, blocks, count, owner, pairs, pair_rest, f, g, first, second, x_ref, y_ref, *rest
):
    outs, held, in_sem, out_sem = rest[:blocks], *rest[blocks:]

    def fetch(source):
        for b in range(blocks):
            pltpu.make_async_copy(
                source.at[pl.ds(b * points, points), :],
                held.at[b, pl.ds(0, points), :],
                in_sem.at[b],
            ).start()

    each_role(lambda: fetch(y_ref), lambda: fetch(x_ref))
    role = lax.axis_index("rep")
    index = lax.axis_index("blk")
    lane = lax.broadcasted_iota(jnp.int32, (1, points), 1)
    listed = jnp.zeros((1, points), jnp.bool_)
    for ref in (pairs, pair_rest):
        for row in range(ref.shape[0]):
            live = ref[row, 0] >= 0
            own = owner[jnp.maximum(ref[row, 0], 0)]
            other = owner[jnp.maximum(ref[row, 1], 0)]
            ahead = lax.rem(other // blocks - index + 2 + count, count)
            code = (ahead * blocks + lax.rem(own, blocks)) * blocks + lax.rem(other, blocks)
            listed = jnp.logical_or(listed, lane == jnp.where(live, code, -1))
    listed = jnp.where(listed, 1.0, 0.0).astype(F32)
    zeros = jnp.zeros((EXTRA - 4, points), F32)
    for b in range(blocks):
        pltpu.make_async_copy(
            x_ref.at[pl.ds(0, points), :], held.at[b, pl.ds(0, points), :], in_sem.at[b]
        ).wait()
        norm = row_norm(held[b, 0:points, :], SCALE / dim)
        potential = jnp.where(role == 0, one_row(g, b, points), one_row(f, b, points))
        mass = jnp.where(role == 0, one_row(second, b, points), one_row(first, b, points))
        terms = in_three(potential * SCALE + jnp.log2(mass) - norm)
        extra = jnp.concatenate([term.astype(F32) for term in terms] + [listed, zeros], 0)
        held[b, points : points + EXTRA, :] = extra.astype(BF16)
        pltpu.make_async_copy(held.at[b], outs[b], out_sem.at[b]).start()
    for b in range(blocks):
        pltpu.make_async_copy(held.at[b], outs[b], out_sem.at[b]).wait()


def spot_of(name, p, blocks):
    place = lax.rem(lax.axis_index("blk"), 4)
    even = lax.rem(place, 2) == 0
    lower = place < 2
    d = {
        "X": jnp.where(even, 1, -1),
        "M": jnp.where(even, -1, 1),
        "Y": jnp.where(lower, 2, -2),
        "Z": jnp.where(lower, -2, 2),
    }[name[0]]
    b = int(name[1])
    return ((d + 2) * blocks + p) * blocks + b, ((2 - d) * blocks + b) * blocks + p


def build_kernel(names, first, last, dim, points, blocks, listing, x_ref, y_ref, *rest):
    rest = list(rest)
    count, home = len(names), names[0][0] == "H"
    state = [rest.pop(0) for _ in range(4)] if first else rest.pop(0)
    if not first:
        del rest[:2]
    sources = [rest.pop(0) for _ in range(count)]
    flags, tiles, high, summed = (rest.pop(0) for _ in range(4))
    if first:
        state_out = rest.pop(0)
    if last:
        packet_out = rest.pop(0)
    own, other, offsets, own_sem, in_sem = rest

    def fetch(source):
        pltpu.make_async_copy(source, own, own_sem).start()

    each_role(lambda: fetch(x_ref), lambda: fetch(y_ref))
    for n in range(count):
        pltpu.make_async_copy(sources[n], other.at[n], in_sem.at[n]).start()
    if first:
        high[...] = jnp.full_like(high, FLOOR)
        summed[...] = jnp.zeros_like(summed)
    factor = 2.0 * SCALE / dim
    role = lax.axis_index("rep")
    lane = lax.broadcasted_iota(jnp.int32, (1, LANES), 1)
    for n, name in enumerate(names):
        extra = sources[n][points : points + EXTRA, :].astype(F32)
        offsets[n : n + 1, :] = extra[0:1, :] + extra[1:2, :] + extra[2:3, :]
        for p in range(blocks):
            if home:
                flags[n * blocks + p] = jnp.int32(p == int(name[1]))
                continue
            as_row, as_col = spot_of(name, p, blocks)
            row = jnp.where(role == 0, listing[0:1, :], extra[3:4, 0:LANES])
            spot = jnp.where(role == 0, as_row, as_col)
            found = jnp.max(jnp.where(lane == spot, row, 0.0))
            flags[n * blocks + p] = found.astype(jnp.int32)
    for n in range(count):
        pltpu.make_async_copy(sources[n], other.at[n], in_sem.at[n]).wait()
    pltpu.make_async_copy(x_ref, own, own_sem).wait()

    def visit(t, _):
        n, p = t // blocks, lax.rem(t, blocks)

        @pl.when(flags[t] > 0)
        def _():
            tile = tiles.at[n if home else t]
            rows = pl.ds(pl.multiple_of(p * points, points), points)
            product = lax.dot_general(
                own[rows, :],
                other[n, 0:points, :],
                (((1,), (1,)), ((), ())),
                preferred_element_type=F32,
            )
            tile[...] = product * factor
            fold_tile(tile, offsets[pl.ds(n, 1), :], high, summed, p * points)

        return 0

    lax.fori_loop(0, count * blocks, visit, 0)
    if first:
        norms = [
            row_norm(own[b * points : (b + 1) * points, :], SCALE / dim) for b in range(blocks)
        ]
        for b in range(blocks):
            potential = jnp.where(
                role == 0, one_row(state[0], b, points), one_row(state[1], b, points)
            )
            mass = jnp.where(
                role == 0, one_row(state[2], b, points), one_row(state[3], b, points)
            )
            state_out[b : b + 1, :] = potential
            state_out[2 * blocks + b : 2 * blocks + b + 1, :] = jnp.log2(mass)
            state_out[blocks + b : blocks + b + 1, :] = norms[b]
    if last:
        _, logs = finish(high, summed, points, blocks)
        new, offset = updated(logs, state[...])
        packet_out[0:blocks, :] = offset
        packet_out[blocks : 2 * blocks, :] = new


def sweep_kernel(names, groups, packet_names, apply, points, blocks, state, before, *rest):
    rest = list(rest)
    total_blocks = len(names)
    some_flags = [rest.pop(0) for _ in groups]
    packets = {name: rest.pop(0) for name in packet_names}
    kept = [rest.pop(0) for _ in groups]
    if apply:
        sources = [rest.pop(0) for _ in range(total_blocks)]
        potential_outs = (rest.pop(0), rest.pop(0))
        mapped_outs = (rest.pop(0), rest.pop(0))
        send_out = rest.pop(0)
        kept = [rest.pop(0) for _ in groups]
        other, sums, halves, peaks, other_sem, half_sem = (rest.pop(0) for _ in range(6))
        for n in range(total_blocks):
            pltpu.make_async_copy(
                sources[n].at[pl.ds(0, points), :], other.at[n], other_sem.at[n]
            ).start()
    else:
        packet_out = rest.pop(0)
    high, summed, offsets = rest
    high[...] = jnp.full_like(high, FLOOR)
    summed[...] = jnp.zeros_like(summed)
    for n, name in enumerate(names):
        b = int(name[1])
        offsets[n : n + 1, :] = packets[name[0]][b : b + 1, :]
    base = 0
    for group, group_flags, tiles in zip(groups, some_flags, kept):
        count, home = len(group), group[0][0] == "H"

        def fold(t, _):
            n, p = t // blocks, lax.rem(t, blocks)

            @pl.when(group_flags[t] > 0)
            def _():
                tile = tiles.at[n if home else t]
                fold_tile(
                    tile,
                    offsets[pl.ds(base + n, 1), :],
                    high,
                    summed,
                    p * points,
                    peaks.at[base * blocks + t] if apply else None,
                    tile if apply else None,
                )

            return 0

        lax.fori_loop(0, count * blocks, fold, 0)
        base += count
    column, logs = finish(high, summed, points, blocks)
    if not apply:
        now = jnp.concatenate([before[blocks : 2 * blocks, :], state[blocks:, :]], 0)
        new, offset = updated(logs, now)
        packet_out[0:blocks, :] = offset
        packet_out[blocks : 2 * blocks, :] = new
        return
    high[...] = jnp.broadcast_to(column, high.shape)
    sums[...] = jnp.zeros_like(sums)
    role = lax.axis_index("rep")
    mine, theirs = before[blocks : 2 * blocks, :], packets["H"][blocks : 2 * blocks, :]
    for out, value in zip(
        potential_outs,
        (jnp.where(role == 0, mine, theirs), jnp.where(role == 0, theirs, mine)),
    ):
        per = points // LANES
        for row in range(out.shape[0]):
            b, l = row // per, row % per
            out[row : row + 1, :] = value[b : b + 1, l * LANES : (l + 1) * LANES]

    base = 0
    for group, group_flags, powers in zip(groups, some_flags, kept):
        count, home = len(group), group[0][0] == "H"

        def weigh(t, _):
            n, p = t // blocks, lax.rem(t, blocks)

            @pl.when(p == 0)
            def _():
                pltpu.make_async_copy(
                    sources[0].at[pl.ds(0, points), :], other.at[base + n], other_sem.at[base + n]
                ).wait()

            @pl.when(group_flags[t] > 0)
            def _():
                rows = pl.ds(pl.multiple_of(p * points, points), points)
                scale = jnp.exp2(peaks[base * blocks + t] - high[rows, :])
                power = powers.at[n if home else t]
                weights = [
                    (power[:, l : l + LANES] * scale).astype(BF16)
                    for l in range(0, points, LANES)
                ]
                sums[rows, :] += jnp.dot(
                    jnp.concatenate(weights, 1), other[base + n], preferred_element_type=F32
                )

            return 0

        lax.fori_loop(0, count * blocks, weigh, 0)
        base += count
    half = sums.shape[1] // 2
    for part in range(2):
        halves[part] = sums[:, part * half : (part + 1) * half].astype(BF16)

    def put(stay, out, leave):
        copies = (
            pltpu.make_async_copy(halves.at[stay], out, half_sem.at[0]),
            pltpu.make_async_copy(halves.at[leave], send_out, half_sem.at[1]),
        )
        for copy in copies:
            copy.start()
        for copy in copies:
            copy.wait()

    each_role(lambda: put(0, mapped_outs[0], 1), lambda: put(1, mapped_outs[1], 0))


def place_kernel(came, x_in, y_in, x_out, y_out, sem):
    def put(out):
        copy = pltpu.make_async_copy(came, out, sem)
        copy.start()
        copy.wait()

    each_role(lambda: put(y_out), lambda: put(x_out))


VMEM_SPEC = pl.BlockSpec(memory_space=pltpu.VMEM)
ANY_SPEC = pl.BlockSpec(memory_space=pl.ANY)
SMEM_SPEC = pl.BlockSpec(memory_space=pltpu.SMEM)


def cost(tiles, points, dim, products):
    area = points * points
    return pl.CostEstimate(
        flops=tiles * area * (2 * dim * products + 8),
        transcendentals=tiles * area,
        bytes_accessed=tiles * area * 4,
    )


def prepare(owner, pairs, pair_rest, vectors, x_points, y_points, points, count):
    rows, dim = x_points.shape
    blocks = rows // points
    payload = (points + EXTRA, dim)
    return pl.pallas_call(
        functools.partial(prepare_kernel, dim, points, blocks, count),
        out_shape=[jax.ShapeDtypeStruct(payload, BF16)] * blocks,
        in_specs=[SMEM_SPEC] * 3 + [VMEM_SPEC] * 4 + [ANY_SPEC] * 2,
        out_specs=[ANY_SPEC] * blocks,
        scratch_shapes=[
            pltpu.VMEM((blocks,) + payload, BF16),
            pltpu.SemaphoreType.DMA((blocks,)),
            pltpu.SemaphoreType.DMA((blocks,)),
        ],
    )(owner, pairs, pair_rest, *vectors, x_points, y_points)


def build(names, listing, x_points, y_points, state, sources, carried, last, points):
    count, home = len(names), names[0][0] == "H"
    rows, dim = x_points.shape
    blocks = rows // points
    tile_count = count if home else count * blocks
    outs = [
        jax.ShapeDtypeStruct((count * blocks,), jnp.int32),
        pltpu.VMEM((tile_count, points, points), F32),
        pltpu.VMEM((rows, LANES), F32),
        pltpu.VMEM((rows, LANES), F32),
    ]
    if home:
        outs.append(pltpu.VMEM((3 * blocks, points), F32))
    if last:
        outs.append(pltpu.VMEM((2 * blocks, points), F32))
    carried = [in_vmem(a) for a in carried or ()]
    start = 3 + len(state)
    return pl.pallas_call(
        functools.partial(build_kernel, names, home, last, dim, points, blocks),
        out_shape=outs,
        in_specs=[VMEM_SPEC, ANY_SPEC, ANY_SPEC]
        + [VMEM_SPEC] * (len(state) + len(carried) + count),
        out_specs=[SMEM_SPEC] + [VMEM_SPEC] * (len(outs) - 1),
        scratch_shapes=[
            pltpu.VMEM((rows, dim), BF16),
            pltpu.VMEM((count, points + EXTRA, dim), BF16),
            pltpu.VMEM((16, points), F32),
            pltpu.SemaphoreType.DMA,
            pltpu.SemaphoreType.DMA((count,)),
        ],
        input_output_aliases={start + n: 2 + n for n in range(len(carried))},
        cost_estimate=cost(tile_count, points, dim, 1),
        compiler_params=pltpu.CompilerParams(vmem_limit_bytes=BUILD_LIMIT),
    )(listing, x_points, y_points, *state, *carried, *[in_vmem(a) for a in sources])


def sweep(names, groups, state, before, flags, packets, kept, sources, rows, dim):
    points = kept[0].shape[1]
    blocks = rows // points
    total_blocks = len(names)
    slots = total_blocks * blocks
    apply = sources is not None
    scratch = []
    if apply:
        half = jax.ShapeDtypeStruct((rows, dim // 2), BF16)
        line = jax.ShapeDtypeStruct((rows // LANES, LANES), F32)
        outs = [line, line, half, half, half]
        outs += [pltpu.VMEM(a.shape, a.dtype) for a in kept]
        out_specs = [VMEM_SPEC] * 2 + [ANY_SPEC] * 3 + [VMEM_SPEC] * len(kept)
        scratch = [
            pltpu.VMEM((total_blocks, points, dim), BF16),
            pltpu.VMEM((rows, dim), F32),
            pltpu.VMEM((2, rows, dim // 2), BF16),
            pltpu.VMEM((slots, points, LANES), F32),
            pltpu.SemaphoreType.DMA((total_blocks,)),
            pltpu.SemaphoreType.DMA((2,)),
        ]
    else:
        outs = [pltpu.VMEM((2 * blocks, points), F32)]
        out_specs = [VMEM_SPEC]
    scratch += [
        pltpu.VMEM((rows, LANES), F32),
        pltpu.VMEM((rows, LANES), F32),
        pltpu.VMEM((16, points), F32),
    ]
    packet_names = sorted(packets)
    return pl.pallas_call(
        functools.partial(sweep_kernel, names, groups, packet_names, apply, points, blocks),
        out_shape=outs,
        in_specs=[VMEM_SPEC] * 2
        + [SMEM_SPEC] * len(flags)
        + [VMEM_SPEC] * (len(packet_names) + len(kept))
        + [ANY_SPEC] * (total_blocks if apply else 0),
        out_specs=out_specs,
        scratch_shapes=scratch,
        input_output_aliases=(
            {2 + len(flags) + len(packet_names) + n: 5 + n for n in range(len(kept))}
            if apply
            else {}
        ),
        cost_estimate=cost(slots, points, dim, 1 if apply else 0),
        compiler_params=pltpu.CompilerParams(
            vmem_limit_bytes=APPLY_LIMIT if apply else SWEEP_LIMIT
        ),
    )(
        in_vmem(state),
        in_vmem(before),
        *flags,
        *[in_vmem(packets[n]) for n in packet_names],
        *[in_vmem(a) for a in kept],
        *(sources or ()),
    )


def placed_beside(came, x_part, y_part):
    shape = jax.ShapeDtypeStruct(came.shape, came.dtype)
    return pl.pallas_call(
        place_kernel,
        out_shape=[shape, shape],
        in_specs=[VMEM_SPEC] + [ANY_SPEC] * 2,
        out_specs=[ANY_SPEC] * 2,
        scratch_shapes=[pltpu.SemaphoreType.DMA],
        input_output_aliases={1: 0, 2: 1},
    )(in_vmem(came), x_part, y_part)


GROUPS = (("H0", "H1"), ("Y0", "X1"), ("X0", "Y1", "Z0"), ("Z1", "M0", "M1"))
ORDER = sum(GROUPS, ())


def per_device(
    x_points, y_points, first_masses, second_masses, f_start, g_start, block_owner, pair_list
):
    count = lax.axis_size("blk")
    rows, dim = x_points.shape
    blocks = block_owner.shape[0] // count
    points = rows // blocks
    place = lax.axis_index("blk") % 4
    vectors = [
        a.reshape(rows // LANES, LANES) for a in (f_start, g_start, first_masses, second_masses)
    ]
    pair_rest = swap(pair_list)
    home = prepare(block_owner, pair_list, pair_rest, vectors, x_points, y_points, points, count)

    y0 = send(home[0], to_y)
    x1 = send(home[1], to_x)
    x0 = send(home[0], to_x)
    y1 = send(home[1], to_y)
    outer = (place == 0) | (place == 3)
    z0 = send(y0, to_z)
    w1 = send(x1, to_z_back, (1, 2))
    m0 = send(jnp.where(outer, y0, z0), to_x)
    m1 = send(jnp.where(outer, x1, w1), to_y)
    z1 = send(y1, to_z)
    arrived = dict(
        H0=home[0], H1=home[1], X0=x0, X1=x1, Y0=y0, Y1=y1, Z0=z0, Z1=z1, M0=m0, M1=m1
    )
    listing = home[0][points + 3 : points + 4, :LANES].astype(F32)

    kept, flags = [], []
    carried, state = None, vectors
    for n, names in enumerate(GROUPS):
        last = n == len(GROUPS) - 1
        out = build(
            names,
            listing,
            x_points,
            y_points,
            state,
            [arrived[name] for name in names],
            carried,
            last,
            points,
        )
        flags.append(out[0])
        kept.append(out[1])
        carried = out[2:4]
        if n == 0:
            state = [in_vmem(out[4])]
        if last:
            packet = out[-1]

    (state,) = state
    packets = exchange(packet)
    (packet,) = sweep(ORDER, GROUPS, state, packet, flags, packets, kept, None, rows, dim)
    packets = exchange(packet)
    f, g, x_part, y_part, leave, *_ = sweep(
        ORDER,
        GROUPS,
        state,
        packet,
        flags,
        packets,
        kept,
        [arrived[name] for name in ORDER],
        rows,
        dim,
    )
    mapped_x, mapped_y = placed_beside(swap(leave), x_part, y_part)
    return f.reshape(rows), g.reshape(rows), mapped_x, mapped_y


def solution(mesh):
    placed = (
        P("blk", None),
        P("blk", None),
        P("blk"),
        P("blk"),
        P("blk"),
        P("blk"),
        P(),
        P(("blk", "rep"), None),
    )
    return jax.shard_map(
        per_device,
        mesh=mesh,
        in_specs=placed,
        out_specs=(P("blk"), P("blk"), P("blk", "rep"), P("blk", "rep")),
        check_vma=False,
    )
```

```python
import functools
import math

import jax
import jax.numpy as jnp
from jax import lax
from jax.experimental import pallas as pl
from jax.experimental.pallas import tpu as pltpu
from jax.sharding import PartitionSpec as P


EPSILON = 0.05
LOG2E = math.log2(math.e)
SCALE = LOG2E / EPSILON
FLOOR = -1e30
LANES = 128
CHUNK = 64
EXTRA = 16
HALVES = 2
BUILD_LIMIT = 12 << 20
SWEEP_LIMIT = 8 << 20
APPLY_LIMIT = 18 << 20
F32 = jnp.float32
BF16 = jnp.bfloat16


def to_x(k):
    return k ^ 1


def to_y(k):
    return k ^ 2


def to_z(k):
    return k + 4 if k % 4 < 2 else k - 4


def to_z_back(k):
    return k - 4 if k % 4 < 2 else k + 4


def to_m(k):
    return k + 1 if k % 2 == 1 else k - 1


def to_z_direct(k):
    return k + 2 if k % 4 >= 2 else k - 2


def send(value, target, places=range(4)):
    count = lax.axis_size("blk")
    pairs = [(k, target(k) % count) for k in range(count) if k % 4 in places]
    return lax.ppermute(value, "blk", pairs)


def send_across(value, target):
    count = lax.axis_size("blk")
    pairs = []
    for k in range(count):
        pairs.append((2 * k, 2 * (target(k) % count) + 1))
        pairs.append((2 * k + 1, 2 * (target(k) % count)))
    return lax.ppermute(value, ("blk", "rep"), pairs)


def swap(value):
    return lax.ppermute(value, "rep", [(0, 1), (1, 0)])


def in_hbm(value):
    return pltpu.with_memory_space_constraint(value, pltpu.HBM)


def in_vmem(value):
    return pltpu.with_memory_space_constraint(value, pltpu.VMEM)


def exchange(packet):
    came = {}
    for source, target in (("M", to_m), ("Z", to_z_direct), ("X", to_x), ("Y", to_y)):
        came[source] = send_across(packet, target)
    came["H"] = swap(packet)
    return came


def fold_tile(tile, offsets, high, summed, first_row, peaks=None, powers=None):
    lanes = [slice(l, l + LANES) for l in range(0, tile.shape[1], LANES)]
    for c in range(0, tile.shape[0], CHUNK):
        rows = slice(c, c + CHUNK)
        held = pl.ds(pl.multiple_of(first_row + c, CHUNK), CHUNK)
        old = high[held, :]
        logits = [tile[rows, l] + offsets[:, l] for l in lanes]
        new = functools.reduce(jnp.maximum, logits, old)
        total = summed[held, :] * jnp.exp2(old - new)
        for l, z in zip(lanes, logits):
            e = jnp.exp2(z - new)
            total = total + e
            if peaks is not None:
                powers[rows, l] = e
        high[held, :] = new
        summed[held, :] = total
        if peaks is not None:
            peaks[rows, :] = new


def finish(high, summed, points, blocks):
    top = high[...]
    highest = jnp.max(top, axis=1, keepdims=True)
    total = jnp.sum(summed[...] * jnp.exp2(top - highest), axis=1, keepdims=True)
    column = highest + jnp.log2(total)
    wide = jnp.broadcast_to(column, top.shape)
    rows = [
        jnp.transpose(wide[b * points : (b + 1) * points, :])[0:1, :] for b in range(blocks)
    ]
    return column, jnp.concatenate(rows, 0)


def updated(logs, state):
    blocks = logs.shape[0]
    potential, norm, mass = (state[n * blocks : (n + 1) * blocks, :] for n in range(3))
    new = 0.5 * (potential - (logs - norm) * (1.0 / SCALE))
    return new, new * SCALE + mass - norm


def each_role(first, second):
    role = lax.axis_index("rep")
    pl.when(role == 0)(first)
    pl.when(role != 0)(second)


def row_norm(block, factor):
    wide = block.astype(F32)
    square = wide * wide
    part = functools.reduce(
        jnp.add, [square[:, l : l + LANES] for l in range(0, square.shape[1], LANES)]
    )
    return jnp.sum(jnp.transpose(part), axis=0, keepdims=True) * factor


def in_three(value):
    first = value.astype(BF16)
    rest = value - first.astype(F32)
    second = rest.astype(BF16)
    return first, second, (rest - second.astype(F32)).astype(BF16)


def one_row(line, b, points):
    per = points // LANES
    return jnp.concatenate([line[b * per + l : b * per + l + 1, :] for l in range(per)], 1)


def piece(h, points):
    size = points // HALVES
    return pl.ds(h * size, size + (EXTRA if h == HALVES - 1 else 0))


def prepare_kernel(
    dim, points, blocks, count, pairs, pair_rest, owner_ref, f_ref, g_ref, first_ref, second_ref,
    x_ref, y_ref, *rest
):
    outs = rest[: blocks * HALVES]
    state_out, owner, f, g, first, second, in_sem, small_sem = rest[blocks * HALVES :]
    small = [
        pltpu.make_async_copy(source, target, small_sem.at[n])
        for n, (source, target) in enumerate(
            (
                (owner_ref, owner),
                (f_ref, f),
                (g_ref, g),
                (first_ref, first),
                (second_ref, second),
            )
        )
    ]
    for copy in small:
        copy.start()
    size = points // HALVES

    def load(source, b, h):
        n = b * HALVES + h
        return pltpu.make_async_copy(
            source.at[pl.ds(n * size, size), :], outs[n].at[pl.ds(0, size), :], in_sem.at[n]
        )

    def fetch(source):
        for b in range(blocks):
            for h in range(HALVES):
                load(source, b, h).start()

    each_role(lambda: fetch(y_ref), lambda: fetch(x_ref))
    for copy in small:
        copy.wait()
    role = lax.axis_index("rep")
    index = lax.axis_index("blk")
    lane = lax.broadcasted_iota(jnp.int32, (1, points), 1)
    listed = jnp.zeros((1, points), jnp.bool_)
    for ref in (pairs, pair_rest):
        for row in range(ref.shape[0]):
            live = ref[row, 0] >= 0
            own = owner[jnp.maximum(ref[row, 0], 0)]
            other = owner[jnp.maximum(ref[row, 1], 0)]
            ahead = lax.rem(other // blocks - index + 2 + count, count)
            code = (ahead * blocks + lax.rem(own, blocks)) * blocks + lax.rem(other, blocks)
            listed = jnp.logical_or(listed, lane == jnp.where(live, code, -1))
    listed = jnp.where(listed, 1.0, 0.0).astype(F32)
    zeros = jnp.zeros((EXTRA - 4, points), F32)
    for b in range(blocks):
        for h in range(HALVES):
            load(x_ref, b, h).wait()
        norm = jnp.concatenate(
            [
                row_norm(outs[b * HALVES + h][0:size, :], SCALE / dim)
                for h in range(HALVES)
            ],
            1,
        )
        potential = jnp.where(role == 0, one_row(g, b, points), one_row(f, b, points))
        mass = jnp.where(role == 0, one_row(second, b, points), one_row(first, b, points))
        terms = in_three(potential * SCALE + jnp.log2(mass) - norm)
        extra = jnp.concatenate([term.astype(F32) for term in terms] + [listed, zeros], 0)
        outs[b * HALVES + HALVES - 1][size : size + EXTRA, :] = extra.astype(BF16)
        own_potential = jnp.where(role == 0, one_row(f, b, points), one_row(g, b, points))
        own_mass = jnp.where(role == 0, one_row(first, b, points), one_row(second, b, points))
        state_out[b : b + 1, :] = own_potential
        state_out[blocks + b : blocks + b + 1, :] = jnp.zeros((1, points), F32)
        state_out[2 * blocks + b : 2 * blocks + b + 1, :] = jnp.log2(own_mass)


def spot_of(name, p, blocks):
    place = lax.rem(lax.axis_index("blk"), 4)
    even = lax.rem(place, 2) == 0
    lower = place < 2
    d = {
        "X": jnp.where(even, 1, -1),
        "M": jnp.where(even, -1, 1),
        "Y": jnp.where(lower, 2, -2),
        "Z": jnp.where(lower, -2, 2),
    }[name[0]]
    b = int(name[1])
    return ((d + 2) * blocks + p) * blocks + b, ((2 - d) * blocks + b) * blocks + p


def build_kernel(names, first, last, dim, points, blocks, listing, x_ref, y_ref, *rest):
    rest = list(rest)
    count, home = len(names), names[0][0] == "H"
    state = rest.pop(0)
    carried = None if first else (rest.pop(0), rest.pop(0))
    sources = [[rest.pop(0) for _ in range(HALVES)] for _ in range(count)]
    flags, tiles = rest.pop(0), rest.pop(0)
    if first:
        state_out = rest.pop(0)
    if last:
        packet_out = rest.pop(0)
    else:
        carried_out = (rest.pop(0), rest.pop(0))
    own, other, high, summed, offsets, own_sem, lane_sem, in_sem = rest

    def carry(sources, targets):
        return [
            pltpu.make_async_copy(source, target, lane_sem.at[n])
            for n, (source, target) in enumerate(zip(sources, targets))
        ]

    def fetch(source):
        pltpu.make_async_copy(source, own, own_sem).start()

    each_role(lambda: fetch(x_ref), lambda: fetch(y_ref))

    def fill(n, h):
        return pltpu.make_async_copy(
            sources[n][h], other.at[n, piece(h, points), :], in_sem.at[n, h]
        )

    for n in range(count):
        for h in range(HALVES):
            fill(n, h).start()
    if first:
        high[...] = jnp.full_like(high, FLOOR)
        summed[...] = jnp.zeros_like(summed)
    else:
        for copy in carry(carried, (high, summed)):
            copy.start()
    factor = 2.0 * SCALE / dim
    role = lax.axis_index("rep")
    lane = lax.broadcasted_iota(jnp.int32, (1, LANES), 1)
    for n, name in enumerate(names):
        extra = sources[n][-1][points // HALVES :, :].astype(F32)
        offsets[n : n + 1, :] = extra[0:1, :] + extra[1:2, :] + extra[2:3, :]
        for p in range(blocks):
            if home:
                flags[n * blocks + p] = jnp.int32(p == int(name[1]))
                continue
            as_row, as_col = spot_of(name, p, blocks)
            row = jnp.where(role == 0, listing[0:1, :], extra[3:4, 0:LANES])
            spot = jnp.where(role == 0, as_row, as_col)
            found = jnp.max(jnp.where(lane == spot, row, 0.0))
            flags[n * blocks + p] = found.astype(jnp.int32)
    for n in range(count):
        for h in range(HALVES):
            fill(n, h).wait()
    pltpu.make_async_copy(x_ref, own, own_sem).wait()
    if not first:
        for copy in carry(carried, (high, summed)):
            copy.wait()

    def visit(t, _):
        n, p = t // blocks, lax.rem(t, blocks)

        @pl.when(flags[t] > 0)
        def _():
            tile = tiles.at[n if home else t]
            rows = pl.ds(pl.multiple_of(p * points, points), points)
            product = lax.dot_general(
                own[rows, :],
                other[n, 0:points, :],
                (((1,), (1,)), ((), ())),
                preferred_element_type=F32,
            )
            tile[...] = product * factor
            fold_tile(tile, offsets[pl.ds(n, 1), :], high, summed, p * points)

        return 0

    lax.fori_loop(0, count * blocks, visit, 0)
    if not last:
        for copy in carry((high, summed), carried_out):
            copy.start()
    if first:
        norms = [
            row_norm(own[b * points : (b + 1) * points, :], SCALE / dim) for b in range(blocks)
        ]
        for b in range(blocks):
            for n in (0, 2):
                row = n * blocks + b
                state_out[row : row + 1, :] = state[row : row + 1, :]
            state_out[blocks + b : blocks + b + 1, :] = norms[b]
    if last:
        _, logs = finish(high, summed, points, blocks)
        new, offset = updated(logs, state[...])
        packet_out[0:blocks, :] = offset
        packet_out[blocks : 2 * blocks, :] = new
    else:
        for copy in carry((high, summed), carried_out):
            copy.wait()


def sweep_kernel(names, groups, packet_names, apply, points, blocks, state, before, *rest):
    rest = list(rest)
    total_blocks = len(names)
    some_flags = [rest.pop(0) for _ in groups]
    packets = {name: rest.pop(0) for name in packet_names}
    kept = [rest.pop(0) for _ in groups]
    if apply:
        sources = [[rest.pop(0) for _ in range(HALVES)] for _ in range(total_blocks)]
        potential_outs = (rest.pop(0), rest.pop(0))
        mapped_outs = (rest.pop(0), rest.pop(0))
        send_out = rest.pop(0)
        kept = [rest.pop(0) for _ in groups]
        other, sums, halves, peaks, other_sem, half_sem = (rest.pop(0) for _ in range(6))
        size = points // HALVES

        def fill(source, n, h):
            return pltpu.make_async_copy(
                source.at[pl.ds(0, size), :],
                other.at[n, pl.ds(h * size, size), :],
                other_sem.at[n, h],
            )

        for n in range(total_blocks):
            for h in range(HALVES):
                fill(sources[n][h], n, h).start()
    else:
        packet_out = rest.pop(0)
    high, summed, offsets = rest
    high[...] = jnp.full_like(high, FLOOR)
    summed[...] = jnp.zeros_like(summed)
    for n, name in enumerate(names):
        b = int(name[1])
        offsets[n : n + 1, :] = packets[name[0]][b : b + 1, :]
    base = 0
    for group, group_flags, tiles in zip(groups, some_flags, kept):
        count, home = len(group), group[0][0] == "H"

        def fold(t, _):
            n, p = t // blocks, lax.rem(t, blocks)

            @pl.when(group_flags[t] > 0)
            def _():
                tile = tiles.at[n if home else t]
                fold_tile(
                    tile,
                    offsets[pl.ds(base + n, 1), :],
                    high,
                    summed,
                    p * points,
                    peaks.at[base * blocks + t] if apply else None,
                    tile if apply else None,
                )

            return 0

        lax.fori_loop(0, count * blocks, fold, 0)
        base += count
    column, logs = finish(high, summed, points, blocks)
    if not apply:
        now = jnp.concatenate([before[blocks : 2 * blocks, :], state[blocks:, :]], 0)
        new, offset = updated(logs, now)
        packet_out[0:blocks, :] = offset
        packet_out[blocks : 2 * blocks, :] = new
        return
    high[...] = jnp.broadcast_to(column, high.shape)
    sums[...] = jnp.zeros_like(sums)
    role = lax.axis_index("rep")
    mine, theirs = before[blocks : 2 * blocks, :], packets["H"][blocks : 2 * blocks, :]
    for out, value in zip(
        potential_outs,
        (jnp.where(role == 0, mine, theirs), jnp.where(role == 0, theirs, mine)),
    ):
        per = points // LANES
        for row in range(out.shape[0]):
            b, l = row // per, row % per
            out[row : row + 1, :] = value[b : b + 1, l * LANES : (l + 1) * LANES]

    base = 0
    for group, group_flags, powers in zip(groups, some_flags, kept):
        count, home = len(group), group[0][0] == "H"

        def weigh(t, _):
            n, p = t // blocks, lax.rem(t, blocks)

            @pl.when(p == 0)
            def _():
                for h in range(HALVES):
                    fill(sources[0][h], base + n, h).wait()

            @pl.when(group_flags[t] > 0)
            def _():
                rows = pl.ds(pl.multiple_of(p * points, points), points)
                scale = jnp.exp2(peaks[base * blocks + t] - high[rows, :])
                power = powers.at[n if home else t]
                weights = [
                    (power[:, l : l + LANES] * scale).astype(BF16)
                    for l in range(0, points, LANES)
                ]
                sums[rows, :] += jnp.dot(
                    jnp.concatenate(weights, 1), other[base + n], preferred_element_type=F32
                )

            return 0

        lax.fori_loop(0, count * blocks, weigh, 0)
        base += count
    half = sums.shape[1] // 2
    for part in range(2):
        halves[part] = sums[:, part * half : (part + 1) * half].astype(BF16)

    def put(stay, out, leave):
        copies = (
            pltpu.make_async_copy(halves.at[stay], out, half_sem.at[0]),
            pltpu.make_async_copy(halves.at[leave], send_out, half_sem.at[1]),
        )
        for copy in copies:
            copy.start()
        for copy in copies:
            copy.wait()

    each_role(lambda: put(0, mapped_outs[0], 1), lambda: put(1, mapped_outs[1], 0))


def place_kernel(came, x_in, y_in, x_out, y_out, sem):
    def put(out):
        copy = pltpu.make_async_copy(came, out, sem)
        copy.start()
        copy.wait()

    each_role(lambda: put(y_out), lambda: put(x_out))


VMEM_SPEC = pl.BlockSpec(memory_space=pltpu.VMEM)
ANY_SPEC = pl.BlockSpec(memory_space=pl.ANY)
HBM_SPEC = pl.BlockSpec(memory_space=pltpu.HBM)
SMEM_SPEC = pl.BlockSpec(memory_space=pltpu.SMEM)


def cost(tiles, points, dim, products):
    area = points * points
    return pl.CostEstimate(
        flops=tiles * area * (2 * dim * products + 8),
        transcendentals=tiles * area,
        bytes_accessed=tiles * area * 4,
    )


def prepare(owner, pairs, pair_rest, vectors, x_points, y_points, points, count):
    rows, dim = x_points.shape
    blocks = rows // points
    sizes = [piece(h, points).size for h in range(HALVES)]
    return pl.pallas_call(
        functools.partial(prepare_kernel, dim, points, blocks, count),
        out_shape=[pltpu.VMEM((size, dim), BF16) for size in sizes] * blocks
        + [pltpu.VMEM((3 * blocks, points), F32)],
        in_specs=[SMEM_SPEC] * 2 + [HBM_SPEC] * 7,
        out_specs=[VMEM_SPEC] * (blocks * HALVES + 1),
        scratch_shapes=[pltpu.SMEM(owner.shape, jnp.int32)]
        + [pltpu.VMEM(a.shape, F32) for a in vectors]
        + [pltpu.SemaphoreType.DMA((blocks * HALVES,)), pltpu.SemaphoreType.DMA((5,))],
        compiler_params=pltpu.CompilerParams(vmem_limit_bytes=BUILD_LIMIT),
    )(pairs, pair_rest, *[in_hbm(a) for a in (owner, *vectors, x_points, y_points)])


def build(names, listing, x_points, y_points, state, sources, carried, last, points):
    count, home = len(names), names[0][0] == "H"
    rows, dim = x_points.shape
    blocks = rows // points
    tile_count = count if home else count * blocks
    outs = [
        jax.ShapeDtypeStruct((count * blocks,), jnp.int32),
        pltpu.VMEM((tile_count, points, points), F32),
    ]
    if home:
        outs.append(pltpu.VMEM((3 * blocks, points), F32))
    if last:
        outs.append(pltpu.VMEM((2 * blocks, points), F32))
    in_place = len(outs)
    if not last:
        outs += [pltpu.HBM((rows, LANES), F32)] * 2
    carried = [in_hbm(a) for a in carried or ()]
    return pl.pallas_call(
        functools.partial(build_kernel, names, home, last, dim, points, blocks),
        out_shape=outs,
        in_specs=[VMEM_SPEC, HBM_SPEC, HBM_SPEC]
        + [VMEM_SPEC]
        + [HBM_SPEC] * len(carried)
        + [VMEM_SPEC] * (count * HALVES),
        out_specs=[SMEM_SPEC]
        + [VMEM_SPEC] * (in_place - 1)
        + [HBM_SPEC] * (len(outs) - in_place),
        scratch_shapes=[
            pltpu.VMEM((rows, dim), BF16),
            pltpu.VMEM((count, points + EXTRA, dim), BF16),
            pltpu.VMEM((rows, LANES), F32),
            pltpu.VMEM((rows, LANES), F32),
            pltpu.VMEM((16, points), F32),
            pltpu.SemaphoreType.DMA,
            pltpu.SemaphoreType.DMA((2,)),
            pltpu.SemaphoreType.DMA((count, HALVES)),
        ],
        cost_estimate=cost(tile_count, points, dim, 1),
        compiler_params=pltpu.CompilerParams(vmem_limit_bytes=BUILD_LIMIT),
    )(listing, in_hbm(x_points), in_hbm(y_points), in_vmem(state), *carried, *[in_vmem(a) for pieces in sources for a in pieces])


def sweep(names, groups, state, before, flags, packets, kept, sources, rows, dim):
    points = kept[0].shape[1]
    blocks = rows // points
    total_blocks = len(names)
    slots = total_blocks * blocks
    apply = sources is not None
    scratch = []
    if apply:
        half = jax.ShapeDtypeStruct((rows, dim // 2), BF16)
        line = jax.ShapeDtypeStruct((rows // LANES, LANES), F32)
        outs = [line, line, half, half, half]
        outs += [pltpu.VMEM(a.shape, a.dtype) for a in kept]
        out_specs = [VMEM_SPEC] * 2 + [ANY_SPEC] * 3 + [VMEM_SPEC] * len(kept)
        scratch = [
            pltpu.VMEM((total_blocks, points, dim), BF16),
            pltpu.VMEM((rows, dim), F32),
            pltpu.VMEM((2, rows, dim // 2), BF16),
            pltpu.VMEM((slots, points, LANES), F32),
            pltpu.SemaphoreType.DMA((total_blocks, HALVES)),
            pltpu.SemaphoreType.DMA((2,)),
        ]
    else:
        outs = [pltpu.VMEM((2 * blocks, points), F32)]
        out_specs = [VMEM_SPEC]
    scratch += [
        pltpu.VMEM((rows, LANES), F32),
        pltpu.VMEM((rows, LANES), F32),
        pltpu.VMEM((16, points), F32),
    ]
    packet_names = sorted(packets)
    return pl.pallas_call(
        functools.partial(sweep_kernel, names, groups, packet_names, apply, points, blocks),
        out_shape=outs,
        in_specs=[VMEM_SPEC] * 2
        + [SMEM_SPEC] * len(flags)
        + [VMEM_SPEC] * (len(packet_names) + len(kept))
        + [VMEM_SPEC] * (total_blocks * HALVES if apply else 0),
        out_specs=out_specs,
        scratch_shapes=scratch,
        input_output_aliases=(
            {2 + len(flags) + len(packet_names) + n: 5 + n for n in range(len(kept))}
            if apply
            else {}
        ),
        cost_estimate=cost(slots, points, dim, 1 if apply else 0),
        compiler_params=pltpu.CompilerParams(
            vmem_limit_bytes=APPLY_LIMIT if apply else SWEEP_LIMIT
        ),
    )(
        in_vmem(state),
        in_vmem(before),
        *flags,
        *[in_vmem(packets[n]) for n in packet_names],
        *[in_vmem(a) for a in kept],
        *[in_vmem(a) for pieces in sources or () for a in pieces],
    )


def placed_beside(came, x_part, y_part):
    shape = jax.ShapeDtypeStruct(came.shape, came.dtype)
    return pl.pallas_call(
        place_kernel,
        out_shape=[shape, shape],
        in_specs=[VMEM_SPEC] + [ANY_SPEC] * 2,
        out_specs=[ANY_SPEC] * 2,
        scratch_shapes=[pltpu.SemaphoreType.DMA],
        input_output_aliases={1: 0, 2: 1},
    )(in_vmem(came), x_part, y_part)


GROUPS = (("H0", "H1"), ("Y0", "X1"), ("X0", "Y1", "Z0"), ("Z1", "M0", "M1"))
ORDER = sum(GROUPS, ())


def per_device(
    x_points, y_points, first_masses, second_masses, f_start, g_start, block_owner, pair_list
):
    count = lax.axis_size("blk")
    rows, dim = x_points.shape
    blocks = block_owner.shape[0] // count
    points = rows // blocks
    place = lax.axis_index("blk") % 4
    vectors = [
        a.reshape(rows // LANES, LANES) for a in (f_start, g_start, first_masses, second_masses)
    ]
    pair_rest = swap(pair_list)
    *home, state = prepare(
        block_owner, pair_list, pair_rest, vectors, x_points, y_points, points, count
    )

    outer = (place == 0) | (place == 3)
    arrived = {"H%d" % b: home[b * HALVES : (b + 1) * HALVES] for b in range(blocks)}
    for name in ("X0", "X1", "Y0", "Y1", "Z0", "Z1", "M0", "M1"):
        arrived[name] = []
    for h in range(HALVES):
        first, second = arrived["H0"][h], arrived["H1"][h]
        y0, x1 = send(first, to_y), send(second, to_x)
        x0, y1 = send(first, to_x), send(second, to_y)
        z0, w1 = send(y0, to_z), send(x1, to_z_back, (1, 2))
        m0 = send(jnp.where(outer, y0, z0), to_x)
        m1 = send(jnp.where(outer, x1, w1), to_y)
        z1 = send(y1, to_z)
        for name, a in dict(X0=x0, X1=x1, Y0=y0, Y1=y1, Z0=z0, Z1=z1, M0=m0, M1=m1).items():
            arrived[name].append(a)
    row = points // HALVES + 3
    listing = arrived["H0"][-1][row : row + 1, :LANES].astype(F32)

    kept, flags = [], []
    carried = None
    for n, names in enumerate(GROUPS):
        last = n == len(GROUPS) - 1
        out = build(
            names,
            listing,
            x_points,
            y_points,
            state,
            [arrived[name] for name in names],
            carried,
            last,
            points,
        )
        flags.append(out[0])
        kept.append(out[1])
        carried = out[-2:]
        if n == 0:
            state = out[2]
        if last:
            packet = out[-1]

    packets = exchange(packet)
    (packet,) = sweep(ORDER, GROUPS, state, packet, flags, packets, kept, None, rows, dim)
    packets = exchange(packet)
    f, g, x_part, y_part, leave, *_ = sweep(
        ORDER,
        GROUPS,
        state,
        packet,
        flags,
        packets,
        kept,
        [arrived[name] for name in ORDER],
        rows,
        dim,
    )
    mapped_x, mapped_y = placed_beside(swap(leave), x_part, y_part)
    return f.reshape(rows), g.reshape(rows), mapped_x, mapped_y


def solution(mesh):
    placed = (
        P("blk", None),
        P("blk", None),
        P("blk"),
        P("blk"),
        P("blk"),
        P("blk"),
        P(),
        P(("blk", "rep"), None),
    )
    return jax.shard_map(
        per_device,
        mesh=mesh,
        in_specs=placed,
        out_specs=(P("blk"), P("blk"), P("blk", "rep"), P("blk", "rep")),
        check_vma=False,
    )
```
